512 devices in a mesh: snp: 32 (over y, x, core), ind: 16 (over z).
Axes of the slice: x: 4, y: 4, z: 16, core: 2. Of those that a mesh axis runs over, the one named last changes fastest.
Arguments:
- genotypes: bfloat16 [32768, 16384], P('ind', 'snp'), may hold values from -12 to 12, as said below
- annotations: bfloat16 [16384, 512], P('snp'), may hold values from -0.3984375 to 0.3984375
- window_start: int32 [16384], P(('snp', 'ind')), may hold values from 0 to 16383, as said below
- window_end: int32 [16384], P(('snp', 'ind')), may hold values from 1 to 16384, as said below
Outputs:
- ld_scores: float32 [16384, 512], P(('snp', 'ind'))
The draws below stay inside these ranges and needn't reach their ends.
Inputs may be any that keep to these rules, and one draw needn't show every extreme that they name: `genotypes`: real-valued dosages, each SNP with its own scale; values within the range. For each SNP j: window_start(j) <= j; j - window_start(j) <= 512, reached on every draw; k is in the window of j exactly when j is in the window of k; never falls along the SNPs. For each SNP j: window_end(j) > j; window_end(j) - j <= 513, reached on every draw; never falls along the SNPs.
All inputs are finite; a program needn't handle non-finite values.
Results may differ from the reference program's by a relative error of at most 0.0033.
Values may be sent and summed in bfloat16 or wider, within the bound.
A program may use at most 64 MiB of HBM per device.

```python
import jax
import jax.numpy as jnp
from jax import lax

S_DEV = 512
C = 512
SNPS = 16384
IND = 32768
N_SNP = 32


def draw_genotypes(key, part):
    subkeys = jax.random.split(key, 7)
    fine_len = S_DEV // 4
    fine_count = SNPS // fine_len + 2
    coarse_count = SNPS // S_DEV + 2
    shift_fine = jax.random.randint(subkeys[0], (), 0, fine_len)
    shift_coarse = jax.random.randint(subkeys[1], (), 0, S_DEV)
    indices = jnp.arange(SNPS, dtype=jnp.int32)
    fine_id = (indices + shift_fine) // fine_len
    coarse_id = (indices + shift_coarse) // S_DEV
    fine_latent = jax.random.normal(subkeys[2], (IND, fine_count), jnp.float32)
    coarse_latent = jax.random.normal(subkeys[3], (IND, coarse_count), jnp.float32)
    w_fine = jax.random.uniform(subkeys[4], (SNPS,), jnp.float32, 0.5, 1.5)
    w_coarse = jax.random.uniform(subkeys[5], (SNPS,), jnp.float32, 0.3, 1.0)
    noise_part = jax.random.normal(subkeys[6], (IND, SNPS), jnp.float32)
    values = fine_latent[:, fine_id] * w_fine + coarse_latent[:, coarse_id] * w_coarse + noise_part
    values = jnp.clip(values, -12.0, 12.0)
    return values.astype(jnp.bfloat16)


def window_bounds(key):
    first_key, second_key = jax.random.split(jax.random.fold_in(key, 11))
    increments = jax.random.randint(first_key, (SNPS,), 0, 4)
    cold_start = jax.random.randint(second_key, (), 0, SNPS - 2 * S_DEV - 1)
    indices = jnp.arange(SNPS, dtype=jnp.int32)
    increments = jnp.where((indices >= cold_start) & (indices <= cold_start + 2 * S_DEV), 0, increments)
    map_pos = jnp.cumsum(increments).astype(jnp.int32)
    map_unit = S_DEV // 2
    lower_edge = jnp.searchsorted(map_pos, map_pos - map_unit, side='left').astype(jnp.int32)
    upper_edge = jnp.searchsorted(map_pos, map_pos + map_unit, side='right').astype(jnp.int32)
    start_out = jnp.maximum(lower_edge, indices - S_DEV)
    end_out = jnp.minimum(upper_edge, indices + S_DEV + 1)
    return (start_out.astype(jnp.int32), end_out.astype(jnp.int32))


def draw_window_start(key, part):
    return window_bounds(key)[0]


def draw_window_end(key, part):
    return window_bounds(key)[1]


def block_scale(stream_key, dims, cuts, smallest, high):
    def one(dim, shards_of):
        heights = jax.random.uniform(jax.random.fold_in(jax.random.fold_in(stream_key, 6), dim), (shards_of,), jnp.float32, smallest / len(cuts), high / len(cuts))
        return jnp.repeat(jnp.exp(heights), dims[dim] // shards_of).reshape((-1,) + (1,) * (len(dims) - dim - 1))

    loudness = one(*cuts[0])
    for cut in cuts[1:]:
        loudness = loudness * one(*cut)
    return loudness


def normal_values(key, dims, scale, reach, pieces=(), kind=jnp.bfloat16):
    values = jax.random.normal(key, dims, jnp.float32) * scale
    if len(pieces) > 0:
        values = block_scale(key, dims, pieces, -0.22, 0.18) * values
    return jnp.clip(values, min=-reach, max=reach).astype(kind)


def setup_inputs(seed: int = 0) -> dict:
    keys = jax.random.split(jax.random.key(seed), 5)
    return {
        "genotypes": draw_genotypes(jax.random.fold_in(keys[4], 71), 0),
        "annotations": normal_values(keys[1], (SNPS, C), 0.0625, 0.3984375, ((0, 32),)),
        "window_start": draw_window_start(jax.random.fold_in(keys[4], 71), 0),
        "window_end": draw_window_end(jax.random.fold_in(keys[4], 71), 0),
    }


def adjust_block(gram_tile, row_sumsq, col_sumsq, col_ids, start_rows, end_rows, count_all):
    col_safe = jnp.where(col_sumsq > 0.0, col_sumsq, 1.0)
    corr_value = gram_tile * lax.rsqrt(row_sumsq)[:, None] * lax.rsqrt(col_safe)[None, :]
    squared = corr_value * corr_value
    adjusted = squared - (1.0 - squared) / (count_all - 2.0)
    inside = (col_ids[None, :] >= start_rows[:, None]) & (col_ids[None, :] < end_rows[:, None])
    return jnp.where(inside, adjusted, 0.0).astype(jnp.bfloat16)

def reference(genotypes, annotations, window_start, window_end):
    geno_pad = jnp.pad(genotypes, ((0, 0), (S_DEV, S_DEV)))
    annot_pad = jnp.pad(annotations, ((S_DEV, S_DEV), (0, 0)))
    count_all = float(IND)

    def one_stripe(stripe_id):
        row_first = (stripe_id * S_DEV).astype(jnp.int32)
        row_block = lax.dynamic_slice_in_dim(genotypes, row_first, S_DEV, 1).astype(jnp.float32)
        col_block = lax.dynamic_slice_in_dim(geno_pad, row_first, 3 * S_DEV, 1).astype(jnp.float32)
        gram_tile = jnp.dot(row_block.T, col_block, precision=lax.Precision.HIGHEST)
        col_sumsq = lax.optimization_barrier(jnp.sum(col_block * col_block, axis=0))
        row_sumsq = lax.optimization_barrier(jnp.sum(row_block * row_block, axis=0))
        col_ids = row_first - S_DEV + jnp.arange(3 * S_DEV, dtype=jnp.int32)
        start_rows = lax.dynamic_slice_in_dim(window_start, row_first, S_DEV, 0)
        end_rows = lax.dynamic_slice_in_dim(window_end, row_first, S_DEV, 0)
        weights = adjust_block(gram_tile, row_sumsq, col_sumsq, col_ids, start_rows, end_rows, count_all)
        annot_block = lax.dynamic_slice_in_dim(annot_pad, row_first, 3 * S_DEV, 0)
        return jnp.dot(weights, annot_block, preferred_element_type=jnp.float32)
    blocks = lax.map(one_stripe, jnp.arange(N_SNP, dtype=jnp.int32))
    return blocks.reshape(SNPS, C)
```

```python
import functools

import jax
import jax.numpy as jnp
from jax import lax
from jax.experimental import pallas as pl
from jax.experimental.pallas import tpu as pltpu
from jax.sharding import PartitionSpec as P

MESH = pl.DeviceIdType.MESH
BF16, F32 = jnp.bfloat16, jnp.float32


def tdot(left, right):
    return lax.dot_general(left, right, (((0,), (0,)), ((), ())), preferred_element_type=F32)


def mm(left, right):
    return jnp.dot(left, right, preferred_element_type=F32)


def safe_rsqrt(v):
    return lax.rsqrt(jnp.where(v > 0.0, v, 1.0))


def kernel(count_all, snps, geno, annot, first, last, out,
           x_v, l0, r1, a_own, a_prev, a_next,
           s1, s2, s3, g1, g2, g3, ss_own, ss_all, ss_tot, ss_side,
           p1, p2, p3, t1, t2, t3,
           x_sem, a_sem, halo_send, halo_recv, ring,
           ss_send, ss_recv, side_send, side_recv,
           g_send, g_recv1, g_recv2, g_recv3, t_send, t_recv1, t_recv2, t_recv3):
    s = lax.axis_index("snp")
    z = lax.axis_index("ind")
    ns, nz = snps, 16
    right, left = lax.rem(s + 1, ns), lax.rem(s + ns - 1, ns)

    def zpeer(d):
        return lax.rem(z + d + nz, nz)

    def rcopy(src, dst, ssem, rsem, dev):
        return pltpu.make_async_remote_copy(
            src_ref=src, dst_ref=dst, send_sem=ssem, recv_sem=rsem,
            device_id=dev, device_id_type=MESH)

    def signal(sem, dev):
        pl.semaphore_signal(sem, inc=1, device_id=dev, device_id_type=MESH)

    x_copy = pltpu.make_async_copy(geno, x_v, x_sem)
    x_copy.start()
    a_copy = pltpu.make_async_copy(annot, a_own, a_sem)
    a_copy.start()

    barrier = pltpu.get_barrier_semaphore()
    signal(barrier, {"snp": left})
    signal(barrier, {"snp": right})
    signal(barrier, {"ind": zpeer(1)})
    signal(barrier, {"ind": zpeer(-1)})
    pl.semaphore_wait(barrier, 4)

    h_left = rcopy(geno.at[:, pl.ds(0, 256)], l0, halo_send.at[0], halo_recv.at[0], {"snp": left})
    h_right = rcopy(geno.at[:, pl.ds(256, 256)], r1, halo_send.at[1], halo_recv.at[1], {"snp": right})
    h_left.start()
    h_right.start()
    ann_l = rcopy(annot, a_next, halo_send.at[2], halo_recv.at[2], {"snp": left})
    ann_r = rcopy(annot, a_prev, halo_send.at[3], halo_recv.at[3], {"snp": right})
    ann_l.start()
    ann_r.start()

    signal(ring.at[0], {"ind": zpeer(1)})
    signal(ring.at[0], {"ind": zpeer(-1)})

    eye = (lax.broadcasted_iota(jnp.int32, (256, 256), 0)
           == lax.broadcasted_iota(jnp.int32, (256, 256), 1))

    x_copy.wait()
    m_lo = tdot(x_v[:, 0:256], x_v[...])
    for b in range(4):
        s1[0:8, b] = m_lo[:, 128 * b:128 * b + 128].reshape(8, 32, 128).astype(BF16)
    ss_own[:, 0:256] = jnp.sum(jnp.where(eye, m_lo[:, 0:256], 0.0), axis=0, keepdims=True)
    pl.semaphore_wait(ring.at[0], 2)
    signal(ring.at[1], {"ind": zpeer(2)})
    signal(ring.at[1], {"ind": zpeer(-2)})
    m_hi = tdot(x_v[:, 256:512], x_v[:, 256:512])
    for b in range(2):
        s1[8:16, 2 + b] = m_hi[:, 128 * b:128 * b + 128].reshape(8, 32, 128).astype(BF16)
    ss_own[:, 256:512] = jnp.sum(jnp.where(eye, m_hi, 0.0), axis=0, keepdims=True)
    pl.semaphore_wait(ring.at[1], 2)
    signal(ring.at[2], {"ind": zpeer(4)})
    signal(ring.at[2], {"ind": zpeer(-4)})
    pl.semaphore_wait(ring.at[2], 2)

    def ss_copy(d):
        dest = lax.rem(z + d, nz)
        return rcopy(ss_own, ss_all.at[z], ss_send.at[d], ss_recv.at[z], {"ind": dest})

    def each_peer(body):
        def step(d, carry):
            body(d)
            return carry
        lax.fori_loop(1, nz, step, 0)

    each_peer(lambda d: ss_copy(d).start())

    def g1_pieces(i, act):
        for g in range(4):
            @pl.when(i // 4 == g)
            def _():
                act(pl.ds(g, 4 - g))

    def g2_pieces(i, act):
        @pl.when(i < 4)
        def _():
            act(pl.ds(0, 1))

        @pl.when(i >= 4)
        def _():
            act(pl.ds(0, 2))

    def g3_pieces(i, act):
        @pl.when((i >= 8) & (i < 12))
        def _():
            act(pl.ds(0, 2))

        @pl.when(i >= 12)
        def _():
            act(pl.ds(1, 1))

    groups = ((s1, g1, g_recv1, g1_pieces, 0), (s2, g2, g_recv2, g2_pieces, 0), (s3, g3, g_recv3, g3_pieces, 8))

    def part_copy(k, d, part):
        src, dst, rsem, _, base = groups[k]
        dest = lax.rem(z + d, nz)
        return rcopy(src.at[dest - base, part], dst.at[z, part], g_send.at[k, d], rsem.at[z], {"ind": dest})

    def part_start(k):
        def body(d):
            groups[k][3](lax.rem(z + d, nz), lambda part: part_copy(k, d, part).start())
        each_peer(body)

    def part_send_wait(k):
        def body(d):
            groups[k][3](lax.rem(z + d, nz), lambda part: part_copy(k, d, part).wait_send())
        each_peer(body)

    def part_recv_wait(k):
        src, dst, rsem, pieces, base = groups[k]

        def body(d):
            origin = lax.rem(z + d, nz)
            pieces(z, lambda part: rcopy(
                dst.at[origin, part], dst.at[origin, part], g_send.at[k, d], rsem.at[origin], {"ind": origin}).wait_recv())
        each_peer(body)

    part_start(0)

    def next_part():
        h_left.wait_recv()
        m2 = tdot(x_v[...], l0[...])
        for b in range(2):
            s2[:, b] = m2[:, 128 * b:128 * b + 128].reshape(16, 32, 128).astype(BF16)
        part_start(1)

    def prev_part():
        h_right.wait_recv()
        m3 = tdot(x_v[:, 256:512], r1[...])
        for b in range(2):
            s3[:, b] = m3[:, 128 * b:128 * b + 128].reshape(8, 32, 128).astype(BF16)
        part_start(2)

    @pl.when(lax.rem(s, 2) == 1)
    def _():
        prev_part()

    next_part()

    @pl.when(lax.rem(s, 2) == 0)
    def _():
        prev_part()

    ss_all[z] = ss_own[...]

    def ss_wait(d):
        origin = lax.rem(z + d, nz)
        rcopy(ss_own, ss_all.at[origin], ss_send.at[d], ss_recv.at[origin], {"ind": origin}).wait_recv()
    each_peer(ss_wait)
    ss_tot[...] = jnp.sum(ss_all[...], axis=0)
    side_l = rcopy(ss_tot, ss_side.at[1], side_send.at[0], side_recv.at[1], {"snp": left})
    side_r = rcopy(ss_tot, ss_side.at[0], side_send.at[1], side_recv.at[0], {"snp": right})
    side_l.start()
    side_r.start()

    def column(row, offset):
        n = row.shape[1]
        hit = (lax.broadcasted_iota(jnp.int32, (32, n), 1)
               == lax.broadcasted_iota(jnp.int32, (32, n), 0) + offset)
        return jnp.sum(jnp.where(hit, jnp.broadcast_to(row, (32, n)), jnp.zeros((), row.dtype)),
                       axis=1, keepdims=True)

    lead = z * 32
    low = column(first[...], 0)
    high = column(last[...], 0)
    row_scale = safe_rsqrt(column(ss_tot[...], lead))

    def weigh(gram, col_ss, col_first, keep):
        n = gram.shape[1]
        corr = gram * row_scale * safe_rsqrt(col_ss)
        squared = corr * corr
        adjusted = squared - (1.0 - squared) / (count_all - 2.0)
        ids = lax.broadcasted_iota(jnp.int32, (32, n), 1) + col_first
        inside = (ids >= low) & (ids < high) & keep
        return jnp.where(inside, adjusted, 0.0).astype(BF16).astype(F32)

    def summed(k, width):
        src, dst, _, pieces, base = groups[k]
        total = dst[0].astype(F32)
        for i in range(1, nz):
            total = total + dst[i].astype(F32)
        return jnp.concatenate([total[b] for b in range(width)], axis=1)

    lane = lax.broadcasted_iota(jnp.int32, (8, 128), 1) // 32

    def pack(weights, buf):
        for b in range(weights.shape[1] // 128):
            for u in range(4):
                tile = jnp.zeros((8, 128), F32)
                for v in range(4):
                    piece = weights[8 * v:8 * v + 8, 128 * b:128 * b + 128]
                    shift = (32 * (v - u)) % 128
                    if shift:
                        piece = pltpu.roll(piece, shift, 1)
                    tile = jnp.where(lane == v, piece, tile)
                buf[4 * b + u] = tile

    rows = lax.broadcasted_iota(jnp.int32, (32, 1), 0) + lead

    def cols(n):
        return lax.broadcasted_iota(jnp.int32, (32, n), 1)

    g1[z] = s1[z]
    part_recv_wait(0)
    gram1 = jnp.where(rows == cols(512), jnp.broadcast_to(ss_tot[...], (32, 512)), summed(0, 4))
    w1 = weigh(gram1, ss_tot[...], s * 512, cols(512) >= lead)
    pack(w1, p1)

    def t1_copy(t):
        return rcopy(p1.at[t], t1.at[z], t_send.at[0, t], t_recv1.at[z], {"ind": t})

    def span(lo, hi, body):
        def step(t, carry):
            @pl.when((t >= lo) & (t < hi))
            def _():
                body(t)
            return carry
        lax.fori_loop(0, nz, step, 0)

    span(z + 1, nz, lambda t: t1_copy(t).start())

    side_l.wait_send()
    side_r.wait_send()
    side_l.wait_recv()
    side_r.wait_recv()
    g2[z] = s2[z]
    part_recv_wait(1)
    w2 = weigh(summed(1, 2), ss_side[1][:, 0:256], (s + 1) * 512, cols(256) <= rows)
    pack(w2, p2)

    def t2_copy(t):
        return rcopy(p2.at[t], t2.at[z], t_send.at[1, t], t_recv2.at[z], {"snp": right, "ind": t})

    span(0, jnp.minimum(z + 1, 8), lambda t: t2_copy(t).start())

    @pl.when(z >= 8)
    def _():
        g3[z] = s3[z - 8]
    part_recv_wait(2)
    w3 = weigh(summed(2, 2), ss_side[0][:, 256:512], s * 512 - 256, (cols(256) + 256 >= rows) & (z >= 8))
    pack(w3, p3)

    def t3_copy(t):
        return rcopy(p3.at[t - 8], t3.at[z - 8], t_send.at[2, t], t_recv3.at[z - 8], {"snp": left, "ind": t})

    t3_first = jnp.where(z >= 8, z, nz)
    span(t3_first, nz, lambda t: t3_copy(t).start())

    a_copy.wait()
    ann_l.wait_recv()
    ann_r.wait_recv()
    score = mm(w1.astype(BF16), a_own[...])
    score = score + mm(w2.astype(BF16), a_next[0:256, :])
    score = score + mm(w3.astype(BF16), a_prev[256:512, :])

    def t_recv_wait(buf, sems, base, i):
        rcopy(buf.at[i - base], buf.at[i - base], t_send.at[0, i], sems.at[i - base], {"ind": i}).wait_recv()

    span(0, z, lambda i: t_recv_wait(t1, t_recv1, 0, i))
    span(jnp.where(z < 8, z, nz), nz, lambda i: t_recv_wait(t2, t_recv2, 0, i))
    span(8, jnp.where(z >= 8, z + 1, 0), lambda i: t_recv_wait(t3, t_recv3, 8, i))

    def spread(buf, lo, hi, base):
        n = buf.shape[0]
        shape = (n, 4, 8, 128)
        tiles = jnp.broadcast_to(buf[...].reshape(n, 1, 8, 128), shape)
        src = lax.broadcasted_iota(jnp.int32, shape, 0) + base
        v = lax.broadcasted_iota(jnp.int32, shape, 1)
        ln = lax.broadcasted_iota(jnp.int32, shape, 3) // 32
        keep = (ln == v) & (src >= lo) & (src < hi)
        return jnp.where(keep, tiles, 0.0).reshape(n * 32, 128).astype(BF16)

    folded = tdot(spread(t1, 0, z, 0), a_own[...])
    folded = folded + tdot(spread(t2, jnp.where(z < 8, z, nz), nz, 0), a_prev[...])
    folded = folded + tdot(spread(t3, 8, jnp.where(z >= 8, z + 1, 0), 8), a_next[256:512, :])
    for v in range(4):
        score = score + folded[32 * v:32 * v + 32, :]
    out[...] = score

    h_left.wait_send()
    h_right.wait_send()
    ann_l.wait_send()
    ann_r.wait_send()
    each_peer(lambda d: ss_copy(d).wait_send())
    for k in range(3):
        part_send_wait(k)
    span(z + 1, nz, lambda t: t1_copy(t).wait_send())
    span(0, jnp.minimum(z + 1, 8), lambda t: t2_copy(t).wait_send())
    span(t3_first, nz, lambda t: t3_copy(t).wait_send())


def per_device(count_all, snps, genotypes, annotations, window_start, window_end):
    dma = pltpu.SemaphoreType.DMA
    vm = pltpu.VMEM
    any_spec = pl.BlockSpec(memory_space=pl.ANY)
    vmem_spec = pl.BlockSpec(memory_space=pltpu.VMEM)
    return pl.pallas_call(
        functools.partial(kernel, count_all, snps),
        out_shape=jax.ShapeDtypeStruct((32, 512), F32),
        in_specs=[any_spec, any_spec, vmem_spec, vmem_spec],
        out_specs=vmem_spec,
        scratch_shapes=[
            vm((2048, 512), BF16), vm((2048, 256), BF16), vm((2048, 256), BF16),
            vm((512, 512), BF16), vm((512, 512), BF16), vm((512, 512), BF16),
            vm((16, 4, 32, 128), BF16), vm((16, 2, 32, 128), BF16), vm((8, 2, 32, 128), BF16),
            vm((16, 4, 32, 128), BF16), vm((16, 2, 32, 128), BF16), vm((16, 2, 32, 128), BF16),
            vm((1, 512), F32), vm((16, 1, 512), F32), vm((1, 512), F32), vm((2, 1, 512), F32),
            vm((16, 8, 128), F32), vm((8, 8, 128), F32), vm((8, 8, 128), F32),
            vm((16, 8, 128), F32), vm((16, 8, 128), F32), vm((8, 8, 128), F32),
            dma, dma, dma((4,)), dma((4,)), pltpu.SemaphoreType.REGULAR((3,)),
            dma((16,)), dma((16,)), dma((2,)), dma((2,)),
            dma((3, 16)), dma((16,)), dma((16,)), dma((16,)),
            dma((3, 16)), dma((16,)), dma((16,)), dma((8,)),
        ],
        compiler_params=pltpu.CompilerParams(
            collective_id=0, has_side_effects=True, vmem_limit_bytes=48 * 1024 * 1024),
        name="ld_scores",
    )(genotypes, annotations, window_start.reshape(1, 32), window_end.reshape(1, 32))


def solution(mesh):
    snps, groups = mesh.shape["snp"], mesh.shape["ind"]
    body = functools.partial(per_device, float(2048 * groups), snps)
    in_specs = (P("ind", "snp"), P("snp", None), P(("snp", "ind")), P(("snp", "ind")))
    return jax.shard_map(
        body, mesh=mesh, in_specs=in_specs, out_specs=P(("snp", "ind"), None), check_vma=False)
```

```python
import functools

import jax
import jax.numpy as jnp
from jax import lax
from jax.experimental import pallas as pl
from jax.experimental.pallas import tpu as pltpu
from jax.sharding import PartitionSpec as P

MESH = pl.DeviceIdType.MESH
BF16, F32 = jnp.bfloat16, jnp.float32


def tdot(left, right):
    return lax.dot_general(left, right, (((0,), (0,)), ((), ())), preferred_element_type=F32)


def mm(left, right):
    return jnp.dot(left, right, preferred_element_type=F32)


def safe_rsqrt(v):
    return lax.rsqrt(jnp.where(v > 0.0, v, 1.0))


def kernel(count_all, snps, geno, annot, first_h, last_h, out,
           x_v, l0, r1, a_own, a_prev, a_next,
           s1, s2, s3, f1, f2, f3, c1, c2, c3, k1, k2, k3, g1, g2, g3, o1, o2, o3, ss_own, ss_all, ss_tot, ss_side,
           p1, p2, p3, t1, t2, t3,
           first, last, win_sem, x_sem, a_sem, halo_send, halo_recv, ring,
           ss_send, ss_recv, side_send, side_recv,
           c_send, c_recv, g_send, g_recv, t_send, t_recv1, t_recv2, t_recv3):
    s = lax.axis_index("snp")
    z = lax.axis_index("ind")
    ns, nz = snps, 16
    right, left = lax.rem(s + 1, ns), lax.rem(s + ns - 1, ns)

    def zpeer(d):
        return lax.rem(z + d + nz, nz)

    def rcopy(src, dst, ssem, rsem, dev):
        return pltpu.make_async_remote_copy(
            src_ref=src, dst_ref=dst, send_sem=ssem, recv_sem=rsem,
            device_id=dev, device_id_type=MESH)

    def signal(sem, dev):
        pl.semaphore_signal(sem, inc=1, device_id=dev, device_id_type=MESH)

    x_copy = pltpu.make_async_copy(geno, x_v, x_sem)
    x_copy.start()
    a_copy = pltpu.make_async_copy(annot, a_own, a_sem)
    a_copy.start()
    f_copy = pltpu.make_async_copy(first_h, first, win_sem.at[0])
    e_copy = pltpu.make_async_copy(last_h, last, win_sem.at[1])
    f_copy.start()
    e_copy.start()

    barrier = pltpu.get_barrier_semaphore()
    signal(barrier, {"snp": left})
    signal(barrier, {"snp": right})
    signal(barrier, {"ind": zpeer(1)})
    signal(barrier, {"ind": zpeer(-1)})
    pl.semaphore_wait(barrier, 4)

    h_left = rcopy(geno.at[:, pl.ds(0, 256)], l0, halo_send.at[0], halo_recv.at[0], {"snp": left})
    h_right = rcopy(geno.at[:, pl.ds(256, 256)], r1, halo_send.at[1], halo_recv.at[1], {"snp": right})
    h_left.start()
    h_right.start()
    ann_l = rcopy(annot, a_next, halo_send.at[2], halo_recv.at[2], {"snp": left})
    ann_r = rcopy(annot, a_prev, halo_send.at[3], halo_recv.at[3], {"snp": right})
    ann_l.start()
    ann_r.start()

    signal(ring.at[0], {"ind": zpeer(1)})
    signal(ring.at[0], {"ind": zpeer(-1)})

    eye = (lax.broadcasted_iota(jnp.int32, (256, 256), 0)
           == lax.broadcasted_iota(jnp.int32, (256, 256), 1))

    def ss_copy(d):
        dest = lax.rem(z + d, nz)
        return rcopy(ss_own, ss_all.at[z], ss_send.at[d], ss_recv.at[z], {"ind": dest})

    def each_peer(body):
        def step(d, carry):
            body(d)
            return carry
        lax.fori_loop(1, nz, step, 0)

    def span(lo, hi, body, top=16):
        def step(t, carry):
            @pl.when((t >= lo) & (t < hi))
            def _():
                body(t)
            return carry
        lax.fori_loop(0, top, step, 0)

    def eight(first_e, body):
        def step(e, carry):
            body(e)
            return carry
        lax.fori_loop(first_e, 8, step, 0)

    even_z = lax.rem(z, 2) == 0
    toward = (jnp.where(even_z, 1, -1), jnp.where(even_z, -1, 1), jnp.where(even_z, -1, 1))
    lows = (0, 0, 8)

    def pieces(k, t, act):
        if k == 0:
            cases = [((t // 4) == g, g, 4 - g) for g in range(4)]
        elif k == 1:
            cases = [(t < 4, 0, 1), (t >= 4, 0, 2)]
        else:
            cases = [((t >= 8) & (t < 12), 0, 2), (t >= 12, 1, 1)]
        for hit, start, size in cases:
            @pl.when(hit)
            def _(start=start, size=size):
                act(pl.ds(start, size))

    sends, wides, gives, sums, ends, owns = (s1, s2, s3), (f1, f2, f3), (c1, c2, c3), (k1, k2, k3), (g1, g2, g3), (o1, o2, o3)

    def give_copy(k, t, part):
        i = t - lows[k]
        return rcopy(sends[k].at[i, part], gives[k].at[i, part], c_send.at[k, t], c_recv.at[k, t],
                     {"ind": zpeer(toward[k])})

    def give(k):
        def body(e):
            t = zpeer(toward[k] * (e + 1))
            pieces(k, t, lambda part: give_copy(k, t, part).start())
        eight(0, body)

    def give_wait(k):
        def body(e):
            t = zpeer(toward[k] * (e + 1))
            pieces(k, t, lambda part: give_copy(k, t, part).wait_send())
        eight(0, body)

    def end_copy(k, e, t, part):
        return rcopy(sums[k].at[t - lows[k], part], ends[k].at[e, part], g_send.at[k, e], g_recv.at[k, e], {"ind": t})

    def combine(k):
        def body(e):
            t = zpeer(-toward[k] * e)
            i = t - lows[k]
            pieces(k, t, lambda part: give_copy(k, t, part).wait_recv())

            def add():
                total = wides[k][i] + gives[k][i].astype(F32)

                @pl.when(e == 0)
                def _():
                    owns[k][...] = total

                @pl.when(e > 0)
                def _():
                    sums[k][i] = total.astype(BF16)
            if lows[k]:
                pl.when(t >= lows[k])(add)
            else:
                add()

        eight(0, body)

        def send(e):
            t = zpeer(-toward[k] * e)
            pieces(k, t, lambda part: end_copy(k, e, t, part).start())
        eight(1, send)

    def end_send_wait(k):
        def body(e):
            t = zpeer(-toward[k] * e)
            pieces(k, t, lambda part: end_copy(k, e, t, part).wait_send())
        eight(1, body)

    def end_recv_wait(k):
        def body(e):
            pieces(k, z, lambda part: rcopy(
                ends[k].at[e, part], ends[k].at[e, part], g_send.at[k, e], g_recv.at[k, e],
                {"ind": zpeer(toward[k])}).wait_recv())
        eight(1, body)

    def keep_blocks(k, gram, rows_at, block_at):
        n = gram.shape[0] // 32
        for b in range(gram.shape[1] // 128):
            tile = gram[:, 128 * b:128 * b + 128].reshape(n, 32, 128)
            wides[k][rows_at:rows_at + n, block_at + b] = tile
            sends[k][rows_at:rows_at + n, block_at + b] = tile.astype(BF16)

    def next_part():
        h_left.wait_recv()
        keep_blocks(1, tdot(x_v[...], l0[...]), 0, 0)
        give(1)

    def prev_part():
        h_right.wait_recv()
        keep_blocks(2, tdot(x_v[:, 256:512], r1[...]), 0, 0)
        give(2)

    odd = lax.rem(s, 2) == 1

    def either(if_odd, if_even):
        pl.when(odd)(if_odd)
        pl.when(jnp.logical_not(odd))(if_even)

    x_copy.wait()
    m_lo = tdot(x_v[:, 0:256], x_v[...])
    keep_blocks(0, m_lo, 0, 0)
    ss_own[:, 0:256] = jnp.sum(jnp.where(eye, m_lo[:, 0:256], 0.0), axis=0, keepdims=True)
    pl.semaphore_wait(ring.at[0], 2)
    signal(ring.at[1], {"ind": zpeer(2)})
    signal(ring.at[1], {"ind": zpeer(-2)})
    m_hi = tdot(x_v[:, 256:512], x_v[:, 256:512])
    keep_blocks(0, m_hi, 8, 2)
    give(0)
    ss_own[:, 256:512] = jnp.sum(jnp.where(eye, m_hi, 0.0), axis=0, keepdims=True)
    pl.semaphore_wait(ring.at[1], 2)
    signal(ring.at[2], {"ind": zpeer(4)})
    signal(ring.at[2], {"ind": zpeer(-4)})
    either(prev_part, next_part)
    pl.semaphore_wait(ring.at[2], 2)
    each_peer(lambda d: ss_copy(d).start())
    combine(0)
    either(lambda: combine(2), lambda: combine(1))
    either(next_part, prev_part)

    ss_all[z] = ss_own[...]

    def ss_wait(d):
        origin = lax.rem(z + d, nz)
        rcopy(ss_own, ss_all.at[origin], ss_send.at[d], ss_recv.at[origin], {"ind": origin}).wait_recv()
    each_peer(ss_wait)
    ss_tot[...] = jnp.sum(ss_all[...], axis=0)
    side_l = rcopy(ss_tot, ss_side.at[1], side_send.at[0], side_recv.at[1], {"snp": left})
    side_r = rcopy(ss_tot, ss_side.at[0], side_send.at[1], side_recv.at[0], {"snp": right})
    side_l.start()
    side_r.start()
    either(lambda: combine(1), lambda: combine(2))

    def column(row, offset):
        n = row.shape[1]
        hit = (lax.broadcasted_iota(jnp.int32, (32, n), 1)
               == lax.broadcasted_iota(jnp.int32, (32, n), 0) + offset)
        return jnp.sum(jnp.where(hit, jnp.broadcast_to(row, (32, n)), jnp.zeros((), row.dtype)),
                       axis=1, keepdims=True)

    lead = z * 32
    f_copy.wait()
    e_copy.wait()
    low = column(first[...], 0)
    high = column(last[...], 0)
    row_scale = safe_rsqrt(column(ss_tot[...], lead))

    def weigh(gram, col_ss, col_first, keep):
        n = gram.shape[1]
        corr = gram * row_scale * safe_rsqrt(col_ss)
        squared = corr * corr
        adjusted = squared - (1.0 - squared) / (count_all - 2.0)
        ids = lax.broadcasted_iota(jnp.int32, (32, n), 1) + col_first
        inside = (ids >= low) & (ids < high) & keep
        return jnp.where(inside, adjusted, 0.0).astype(BF16).astype(F32)

    def summed(k, width):
        total = owns[k][...]
        for e in range(1, 8):
            total = total + ends[k][e].astype(F32)
        return jnp.concatenate([total[b] for b in range(width)], axis=1)

    lane = lax.broadcasted_iota(jnp.int32, (8, 128), 1) // 32

    def pack(weights, buf):
        for b in range(weights.shape[1] // 128):
            for u in range(4):
                tile = jnp.zeros((8, 128), F32)
                for v in range(4):
                    piece = weights[8 * v:8 * v + 8, 128 * b:128 * b + 128]
                    shift = (32 * (v - u)) % 128
                    if shift:
                        piece = pltpu.roll(piece, shift, 1)
                    tile = jnp.where(lane == v, piece, tile)
                buf[4 * b + u] = tile

    rows = lax.broadcasted_iota(jnp.int32, (32, 1), 0) + lead

    def cols(n):
        return lax.broadcasted_iota(jnp.int32, (32, n), 1)

    end_recv_wait(0)
    gram1 = jnp.where(rows == cols(512), jnp.broadcast_to(ss_tot[...], (32, 512)), summed(0, 4))
    w1 = weigh(gram1, ss_tot[...], s * 512, cols(512) >= lead)
    pack(w1, p1)

    def t1_copy(t):
        return rcopy(p1.at[t], t1.at[z], t_send.at[0, t], t_recv1.at[z], {"ind": t})

    span(z + 1, nz, lambda t: t1_copy(t).start())

    side_l.wait_send()
    side_r.wait_send()
    side_l.wait_recv()
    side_r.wait_recv()
    end_recv_wait(1)
    w2 = weigh(summed(1, 2), ss_side[1][:, 0:256], (s + 1) * 512, cols(256) <= rows)
    pack(w2, p2)

    def t2_copy(t):
        return rcopy(p2.at[t], t2.at[z], t_send.at[1, t], t_recv2.at[z], {"snp": right, "ind": t})

    span(0, jnp.minimum(z + 1, 8), lambda t: t2_copy(t).start())

    end_recv_wait(2)
    w3 = weigh(summed(2, 2), ss_side[0][:, 256:512], s * 512 - 256, (cols(256) + 256 >= rows) & (z >= 8))
    pack(w3, p3)

    def t3_copy(t):
        return rcopy(p3.at[t - 8], t3.at[z - 8], t_send.at[2, t], t_recv3.at[z - 8], {"snp": left, "ind": t})

    t3_first = jnp.where(z >= 8, z, nz)
    span(t3_first, nz, lambda t: t3_copy(t).start())

    a_copy.wait()
    ann_l.wait_recv()
    ann_r.wait_recv()
    score = mm(w1.astype(BF16), a_own[...])
    score = score + mm(w2.astype(BF16), a_next[0:256, :])
    score = score + mm(w3.astype(BF16), a_prev[256:512, :])

    def t_recv_wait(buf, sems, base, i):
        rcopy(buf.at[i - base], buf.at[i - base], t_send.at[0, i], sems.at[i - base], {"ind": i}).wait_recv()

    span(0, z, lambda i: t_recv_wait(t1, t_recv1, 0, i))
    span(jnp.where(z < 8, z, nz), nz, lambda i: t_recv_wait(t2, t_recv2, 0, i))
    span(8, jnp.where(z >= 8, z + 1, 0), lambda i: t_recv_wait(t3, t_recv3, 8, i))

    def spread(buf, lo, hi, base):
        n = buf.shape[0]
        shape = (n, 4, 8, 128)
        tiles = jnp.broadcast_to(buf[...].reshape(n, 1, 8, 128), shape)
        src = lax.broadcasted_iota(jnp.int32, shape, 0) + base
        v = lax.broadcasted_iota(jnp.int32, shape, 1)
        ln = lax.broadcasted_iota(jnp.int32, shape, 3) // 32
        keep = (ln == v) & (src >= lo) & (src < hi)
        return jnp.where(keep, tiles, 0.0).reshape(n * 32, 128).astype(BF16)

    folded = tdot(spread(t1, 0, z, 0), a_own[...])
    folded = folded + tdot(spread(t2, jnp.where(z < 8, z, nz), nz, 0), a_prev[...])
    folded = folded + tdot(spread(t3, 8, jnp.where(z >= 8, z + 1, 0), 8), a_next[256:512, :])
    for v in range(4):
        score = score + folded[32 * v:32 * v + 32, :]
    out[...] = score

    h_left.wait_send()
    h_right.wait_send()
    ann_l.wait_send()
    ann_r.wait_send()
    each_peer(lambda d: ss_copy(d).wait_send())
    for k in range(3):
        give_wait(k)
        end_send_wait(k)
    span(z + 1, nz, lambda t: t1_copy(t).wait_send())
    span(0, jnp.minimum(z + 1, 8), lambda t: t2_copy(t).wait_send())
    span(t3_first, nz, lambda t: t3_copy(t).wait_send())


def per_device(count_all, snps, genotypes, annotations, window_start, window_end):
    dma = pltpu.SemaphoreType.DMA
    vm = pltpu.VMEM
    any_spec = pl.BlockSpec(memory_space=pltpu.HBM)
    vmem_spec = pl.BlockSpec(memory_space=pltpu.VMEM)
    return pl.pallas_call(
        functools.partial(kernel, count_all, snps),
        out_shape=jax.ShapeDtypeStruct((32, 512), F32),
        in_specs=[any_spec, any_spec, any_spec, any_spec],
        out_specs=vmem_spec,
        scratch_shapes=[
            vm((2048, 512), BF16), vm((2048, 256), BF16), vm((2048, 256), BF16),
            vm((512, 512), BF16), vm((512, 512), BF16), vm((512, 512), BF16),
            *[vm((n, b, 32, 128), kind) for kind in (BF16, F32, BF16, BF16) for n, b in ((16, 4), (16, 2), (8, 2))],
            *[vm((8, b, 32, 128), BF16) for b in (4, 2, 2)],
            *[vm((b, 32, 128), F32) for b in (4, 2, 2)],
            vm((1, 512), F32), vm((16, 1, 512), F32), vm((1, 512), F32), vm((2, 1, 512), F32),
            vm((16, 8, 128), F32), vm((8, 8, 128), F32), vm((8, 8, 128), F32),
            vm((16, 8, 128), F32), vm((16, 8, 128), F32), vm((8, 8, 128), F32),
            vm((1, 32), jnp.int32), vm((1, 32), jnp.int32), dma((2,)),
            dma, dma, dma((4,)), dma((4,)), pltpu.SemaphoreType.REGULAR((3,)),
            dma((16,)), dma((16,)), dma((2,)), dma((2,)),
            dma((3, 16)), dma((3, 16)), dma((3, 8)), dma((3, 8)),
            dma((3, 16)), dma((16,)), dma((16,)), dma((8,)),
        ],
        compiler_params=pltpu.CompilerParams(
            collective_id=0, has_side_effects=True, vmem_limit_bytes=67043328),
        name="ld_scores",
    )(genotypes, annotations, window_start.reshape(1, 32), window_end.reshape(1, 32))


def solution(mesh):
    snps, groups = mesh.shape["snp"], mesh.shape["ind"]
    body = functools.partial(per_device, float(2048 * groups), snps)
    in_specs = (P("ind", "snp"), P("snp", None), P(("snp", "ind")), P(("snp", "ind")))
    return jax.shard_map(
        body, mesh=mesh, in_specs=in_specs, out_specs=P(("snp", "ind"), None), check_vma=False)
```

```python
import functools

import jax
import jax.numpy as jnp
from jax import lax
from jax.experimental import pallas as pl
from jax.experimental.pallas import tpu as pltpu
from jax.sharding import PartitionSpec as P

MESH = pl.DeviceIdType.MESH
BF16, F32 = jnp.bfloat16, jnp.float32


def tdot(left, right):
    return lax.dot_general(left, right, (((0,), (0,)), ((), ())), preferred_element_type=F32)


def mm(left, right):
    return jnp.dot(left, right, preferred_element_type=F32)


def safe_rsqrt(v):
    return lax.rsqrt(jnp.where(v > 0.0, v, 1.0))


def kernel(count_all, snps, geno, annot, first_h, last_h, out,
           x_v, l0, r1, a_own, a_prev, a_next,
           s1, s2, s3, f1, f2, f3, c1, c2, c3, k1, k2, k3, g1, g2, g3, o1, o2, o3, score_v, folded_v, ss_own, ss_all, ss_tot, ss_side,
           p1, p2, p3, t1, t2, t3,
           first, last, win_sem, x_sem, a_sem, halo_send, halo_recv, ring,
           ss_send, ss_recv, side_send, side_recv,
           c_send, c_recv, g_send, g_recv, t_send, t_recv1, t_recv2, t_recv3):
    s = lax.axis_index("snp")
    z = lax.axis_index("ind")
    ns, nz = snps, 16
    right, left = lax.rem(s + 1, ns), lax.rem(s + ns - 1, ns)

    def zpeer(d):
        return lax.rem(z + d + nz, nz)

    def rcopy(src, dst, ssem, rsem, dev):
        return pltpu.make_async_remote_copy(
            src_ref=src, dst_ref=dst, send_sem=ssem, recv_sem=rsem,
            device_id=dev, device_id_type=MESH)

    def signal(sem, dev):
        pl.semaphore_signal(sem, inc=1, device_id=dev, device_id_type=MESH)

    x_copy = pltpu.make_async_copy(geno, x_v, x_sem)
    x_copy.start()
    a_copy = pltpu.make_async_copy(annot, a_own, a_sem)
    a_copy.start()
    f_copy = pltpu.make_async_copy(first_h, first, win_sem.at[0])
    e_copy = pltpu.make_async_copy(last_h, last, win_sem.at[1])
    f_copy.start()
    e_copy.start()

    barrier = pltpu.get_barrier_semaphore()
    signal(barrier, {"snp": left})
    signal(barrier, {"snp": right})
    signal(barrier, {"ind": zpeer(1)})
    signal(barrier, {"ind": zpeer(-1)})
    pl.semaphore_wait(barrier, 4)

    h_left = rcopy(geno.at[:, pl.ds(0, 256)], l0, halo_send.at[0], halo_recv.at[0], {"snp": left})
    h_right = rcopy(geno.at[:, pl.ds(256, 256)], r1, halo_send.at[1], halo_recv.at[1], {"snp": right})
    h_left.start()
    h_right.start()
    ann_l = rcopy(annot, a_next, halo_send.at[2], halo_recv.at[2], {"snp": left})
    ann_r = rcopy(annot, a_prev, halo_send.at[3], halo_recv.at[3], {"snp": right})
    ann_l.start()
    ann_r.start()

    signal(ring.at[0], {"ind": zpeer(1)})
    signal(ring.at[0], {"ind": zpeer(-1)})

    eye = (lax.broadcasted_iota(jnp.int32, (256, 256), 0)
           == lax.broadcasted_iota(jnp.int32, (256, 256), 1))

    def ss_copy(d):
        dest = lax.rem(z + d, nz)
        return rcopy(ss_own, ss_all.at[z], ss_send.at[d], ss_recv.at[z], {"ind": dest})

    def each_peer(body):
        def step(d, carry):
            body(d)
            return carry
        lax.fori_loop(1, nz, step, 0)

    def span(lo, hi, body, top=16):
        def step(t, carry):
            @pl.when((t >= lo) & (t < hi))
            def _():
                body(t)
            return carry
        lax.fori_loop(0, top, step, 0)

    def eight(first_e, body, end_e=8):
        def step(e, carry):
            body(e)
            return carry
        lax.fori_loop(first_e, end_e, step, 0)

    even_z = lax.rem(z, 2) == 0
    toward = (jnp.where(even_z, 1, -1), jnp.where(even_z, -1, 1), jnp.where(even_z, -1, 1))
    lows = (0, 0, 8)

    def pieces(k, t, act):
        if k == 0:
            cases = [((t // 4) == g, g, 4 - g) for g in range(4)]
        elif k == 1:
            cases = [(t < 4, 0, 1), (t >= 4, 0, 2)]
        else:
            cases = [((t >= 8) & (t < 12), 0, 2), (t >= 12, 1, 1)]
        for hit, start, size in cases:
            @pl.when(hit)
            def _(start=start, size=size):
                act(pl.ds(start, size))

    sends, wides, gives, sums, ends, owns = (s1, s2, s3), (f1, f2, f3), (c1, c2, c3), (k1, k2, k3), (g1, g2, g3), (o1, o2, o3)

    def give_copy(k, t, part):
        i = t - lows[k]
        return rcopy(sends[k].at[i, part], gives[k].at[i, part], c_send.at[k, t], c_recv.at[k, t],
                     {"ind": zpeer(toward[k])})

    def give(k):
        def body(e):
            t = zpeer(toward[k] * (e + 1))
            pieces(k, t, lambda part: give_copy(k, t, part).start())
        eight(0, body)

    def give_wait(k):
        def body(e):
            t = zpeer(toward[k] * (e + 1))
            pieces(k, t, lambda part: give_copy(k, t, part).wait_send())
        eight(0, body)

    def end_copy(k, e, t, part):
        return rcopy(sums[k].at[t - lows[k], part], ends[k].at[e, part], g_send.at[k, e], g_recv.at[k, e], {"ind": t})

    def combine(k, near=0, far=8):
        def body(n):
            e = near + far - 1 - n
            t = zpeer(-toward[k] * e)
            i = t - lows[k]
            pieces(k, t, lambda part: give_copy(k, t, part).wait_recv())

            def add():
                total = wides[k][i] + gives[k][i].astype(F32)

                @pl.when(e == 0)
                def _():
                    owns[k][...] = total

                @pl.when(e > 0)
                def _():
                    sums[k][i] = total.astype(BF16)
            if lows[k]:
                pl.when(t >= lows[k])(add)
            else:
                add()

            def go():
                pieces(k, t, lambda part: end_copy(k, e, t, part).start())
            pl.when(e > 0)(go)

        eight(near, body, far)

    def end_send_wait(k):
        def body(e):
            t = zpeer(-toward[k] * e)
            pieces(k, t, lambda part: end_copy(k, e, t, part).wait_send())
        eight(1, body)

    def end_recv_wait(k):
        def body(e):
            pieces(k, z, lambda part: rcopy(
                ends[k].at[e, part], ends[k].at[e, part], g_send.at[k, e], g_recv.at[k, e],
                {"ind": zpeer(toward[k])}).wait_recv())
        eight(1, body)

    def keep_blocks(k, gram, rows_at, block_at):
        n = gram.shape[0] // 32
        for b in range(gram.shape[1] // 128):
            tile = gram[:, 128 * b:128 * b + 128].reshape(n, 32, 128)
            wides[k][rows_at:rows_at + n, block_at + b] = tile
            sends[k][rows_at:rows_at + n, block_at + b] = tile.astype(BF16)

    def next_part():
        h_left.wait_recv()
        keep_blocks(1, tdot(x_v[...], l0[...]), 0, 0)
        give(1)

    def prev_part():
        h_right.wait_recv()
        keep_blocks(2, tdot(x_v[:, 256:512], r1[...]), 0, 0)
        give(2)

    odd = lax.rem(s, 2) == 1

    def either(if_odd, if_even):
        pl.when(odd)(if_odd)
        pl.when(jnp.logical_not(odd))(if_even)

    pl.semaphore_wait(ring.at[0], 2)
    signal(ring.at[1], {"ind": zpeer(2)})
    signal(ring.at[1], {"ind": zpeer(-2)})
    x_copy.wait()
    m_lo = tdot(x_v[:, 0:256], x_v[...])
    keep_blocks(0, m_lo, 0, 0)
    ss_own[:, 0:256] = jnp.sum(jnp.where(eye, m_lo[:, 0:256], 0.0), axis=0, keepdims=True)
    pl.semaphore_wait(ring.at[1], 2)
    signal(ring.at[2], {"ind": zpeer(4)})
    signal(ring.at[2], {"ind": zpeer(-4)})
    m_hi = tdot(x_v[:, 256:512], x_v[:, 256:512])
    keep_blocks(0, m_hi, 8, 2)
    give(0)
    ss_own[:, 256:512] = jnp.sum(jnp.where(eye, m_hi, 0.0), axis=0, keepdims=True)
    either(prev_part, next_part)
    pl.semaphore_wait(ring.at[2], 2)
    each_peer(lambda d: ss_copy(d).start())
    combine(0)
    either(lambda: combine(2), lambda: combine(1))
    either(next_part, prev_part)

    ss_all[z] = ss_own[...]

    def ss_wait(d):
        origin = lax.rem(z + d, nz)
        rcopy(ss_own, ss_all.at[origin], ss_send.at[d], ss_recv.at[origin], {"ind": origin}).wait_recv()
    each_peer(ss_wait)
    ss_tot[...] = jnp.sum(ss_all[...], axis=0)
    side_l = rcopy(ss_tot, ss_side.at[1], side_send.at[0], side_recv.at[1], {"snp": left})
    side_r = rcopy(ss_tot, ss_side.at[0], side_send.at[1], side_recv.at[0], {"snp": right})
    side_l.start()
    side_r.start()
    either(lambda: combine(1), lambda: combine(2))

    def column(row, offset):
        n = row.shape[1]
        hit = (lax.broadcasted_iota(jnp.int32, (32, n), 1)
               == lax.broadcasted_iota(jnp.int32, (32, n), 0) + offset)
        return jnp.sum(jnp.where(hit, jnp.broadcast_to(row, (32, n)), jnp.zeros((), row.dtype)),
                       axis=1, keepdims=True)

    lead = z * 32
    f_copy.wait()
    e_copy.wait()
    low = column(first[...], 0)
    high = column(last[...], 0)
    row_scale = safe_rsqrt(column(ss_tot[...], lead))

    def weigh(gram, col_ss, col_first, keep):
        n = gram.shape[1]
        corr = gram * row_scale * safe_rsqrt(col_ss)
        squared = corr * corr
        adjusted = squared - (1.0 - squared) / (count_all - 2.0)
        ids = lax.broadcasted_iota(jnp.int32, (32, n), 1) + col_first
        inside = (ids >= low) & (ids < high) & keep
        return jnp.where(inside, adjusted, 0.0).astype(BF16).astype(F32)

    def summed(k, width):
        total = owns[k][...]
        for e in range(1, 8):
            total = total + ends[k][e].astype(F32)
        return jnp.concatenate([total[b] for b in range(width)], axis=1)

    lane = lax.broadcasted_iota(jnp.int32, (8, 128), 1) // 32

    def pack(weights, buf):
        for b in range(weights.shape[1] // 128):
            for u in range(4):
                tile = jnp.zeros((8, 128), F32)
                for v in range(4):
                    piece = weights[8 * v:8 * v + 8, 128 * b:128 * b + 128]
                    shift = (32 * (v - u)) % 128
                    if shift:
                        piece = pltpu.roll(piece, shift, 1)
                    tile = jnp.where(lane == v, piece, tile)
                buf[4 * b + u] = tile.astype(BF16)

    rows = lax.broadcasted_iota(jnp.int32, (32, 1), 0) + lead

    def cols(n):
        return lax.broadcasted_iota(jnp.int32, (32, n), 1)

    end_recv_wait(0)
    gram1 = jnp.where(rows == cols(512), jnp.broadcast_to(ss_tot[...], (32, 512)), summed(0, 4))
    w1 = weigh(gram1, ss_tot[...], s * 512, cols(512) >= lead)
    pack(w1, p1)

    def t1_copy(t):
        return rcopy(p1.at[t], t1.at[z], t_send.at[0, t], t_recv1.at[z], {"ind": t})

    span(z + 1, nz, lambda t: t1_copy(t).start())

    side_l.wait_send()
    side_r.wait_send()
    side_l.wait_recv()
    side_r.wait_recv()
    def t2_copy(t):
        return rcopy(p2.at[t], t2.at[z], t_send.at[1, t], t_recv2.at[z], {"snp": right, "ind": t})

    def t3_copy(t):
        return rcopy(p3.at[t - 8], t3.at[z - 8], t_send.at[2, t], t_recv3.at[z - 8], {"snp": left, "ind": t})

    t3_first = jnp.where(z >= 8, z, nz)
    a_copy.wait()
    ann_l.wait_recv()
    ann_r.wait_recv()
    score_v[...] = mm(w1.astype(BF16), a_own[...])

    def next_own():
        end_recv_wait(1)
        w2 = weigh(summed(1, 2), ss_side[1][:, 0:256], (s + 1) * 512, cols(256) <= rows)
        pack(w2, p2)
        span(0, jnp.minimum(z + 1, 8), lambda t: t2_copy(t).start())
        score_v[...] += mm(w2.astype(BF16), a_next[0:256, :])

    def prev_own():
        end_recv_wait(2)
        w3 = weigh(summed(2, 2), ss_side[0][:, 256:512], s * 512 - 256, (cols(256) + 256 >= rows) & (z >= 8))
        pack(w3, p3)
        span(t3_first, nz, lambda t: t3_copy(t).start())
        score_v[...] += mm(w3.astype(BF16), a_prev[256:512, :])

    either(prev_own, next_own)
    either(next_own, prev_own)

    h_left.wait_send()
    h_right.wait_send()
    ann_l.wait_send()
    ann_r.wait_send()
    each_peer(lambda d: ss_copy(d).wait_send())
    for k in range(3):
        give_wait(k)
        end_send_wait(k)
    span(z + 1, nz, lambda t: t1_copy(t).wait_send())
    span(0, jnp.minimum(z + 1, 8), lambda t: t2_copy(t).wait_send())
    span(t3_first, nz, lambda t: t3_copy(t).wait_send())

    def t_recv_wait(buf, sems, base, i):
        rcopy(buf.at[i - base], buf.at[i - base], t_send.at[0, i], sems.at[i - base], {"ind": i}).wait_recv()

    def spread(buf, lo, hi, base):
        n = buf.shape[0]
        shape = (n, 4, 8, 128)
        tiles = jnp.broadcast_to(buf[...].astype(F32).reshape(n, 1, 8, 128), shape)
        src = lax.broadcasted_iota(jnp.int32, shape, 0) + base
        v = lax.broadcasted_iota(jnp.int32, shape, 1)
        ln = lax.broadcasted_iota(jnp.int32, shape, 3) // 32
        keep = (ln == v) & (src >= lo) & (src < hi)
        return jnp.where(keep, tiles, 0.0).reshape(n * 32, 128).astype(BF16)

    span(0, z, lambda i: t_recv_wait(t1, t_recv1, 0, i))
    folded = tdot(spread(t1, 0, z, 0), a_own[...])
    folded_v[...] = folded
    span(jnp.where(z < 8, z, nz), nz, lambda i: t_recv_wait(t2, t_recv2, 0, i))
    span(8, jnp.where(z >= 8, z + 1, 0), lambda i: t_recv_wait(t3, t_recv3, 8, i))
    score = score_v[...]
    folded = folded_v[...]
    folded = folded + tdot(spread(t2, jnp.where(z < 8, z, nz), nz, 0), a_prev[...])
    folded = folded + tdot(spread(t3, 8, jnp.where(z >= 8, z + 1, 0), 8), a_next[256:512, :])
    for v in range(4):
        score = score + folded[32 * v:32 * v + 32, :]
    out[...] = score


def per_device(count_all, snps, genotypes, annotations, window_start, window_end):
    dma = pltpu.SemaphoreType.DMA
    vm = pltpu.VMEM
    any_spec = pl.BlockSpec(memory_space=pltpu.HBM)
    vmem_spec = pl.BlockSpec(memory_space=pltpu.VMEM)
    return pl.pallas_call(
        functools.partial(kernel, count_all, snps),
        out_shape=jax.ShapeDtypeStruct((32, 512), F32),
        in_specs=[any_spec, any_spec, any_spec, any_spec],
        out_specs=vmem_spec,
        scratch_shapes=[
            vm((2048, 512), BF16), vm((2048, 256), BF16), vm((2048, 256), BF16),
            vm((512, 512), BF16), vm((512, 512), BF16), vm((512, 512), BF16),
            *[vm((n, b, 32, 128), kind) for kind in (BF16, F32, BF16, BF16) for n, b in ((16, 4), (16, 2), (8, 2))],
            *[vm((8, b, 32, 128), BF16) for b in (4, 2, 2)],
            *[vm((b, 32, 128), F32) for b in (4, 2, 2)], vm((32, 512), F32), vm((128, 512), F32),
            vm((1, 512), F32), vm((16, 1, 512), F32), vm((1, 512), F32), vm((2, 1, 512), F32),
            vm((16, 8, 128), BF16), vm((8, 8, 128), BF16), vm((8, 8, 128), BF16),
            vm((16, 8, 128), BF16), vm((16, 8, 128), BF16), vm((8, 8, 128), BF16),
            vm((1, 32), jnp.int32), vm((1, 32), jnp.int32), dma((2,)),
            dma, dma, dma((4,)), dma((4,)), pltpu.SemaphoreType.REGULAR((3,)),
            dma((16,)), dma((16,)), dma((2,)), dma((2,)),
            dma((3, 16)), dma((3, 16)), dma((3, 8)), dma((3, 8)),
            dma((3, 16)), dma((16,)), dma((16,)), dma((8,)),
        ],
        compiler_params=pltpu.CompilerParams(
            collective_id=0, has_side_effects=True, vmem_limit_bytes=67043328),
        name="ld_scores",
    )(genotypes, annotations, window_start.reshape(1, 32), window_end.reshape(1, 32))


def solution(mesh):
    snps, groups = mesh.shape["snp"], mesh.shape["ind"]
    body = functools.partial(per_device, float(2048 * groups), snps)
    in_specs = (P("ind", "snp"), P("snp", None), P(("snp", "ind")), P(("snp", "ind")))
    return jax.shard_map(
        body, mesh=mesh, in_specs=in_specs, out_specs=P(("snp", "ind"), None), check_vma=False)
```

```python
import functools

import jax
import jax.numpy as jnp
from jax import lax
from jax.experimental import pallas as pl
from jax.experimental.pallas import tpu as pltpu
from jax.sharding import PartitionSpec as P

MESH = pl.DeviceIdType.MESH
BF16, F32 = jnp.bfloat16, jnp.float32


def tdot(left, right):
    return lax.dot_general(left, right, (((0,), (0,)), ((), ())), preferred_element_type=F32)


def mm(left, right):
    return jnp.dot(left, right, preferred_element_type=F32)


def safe_rsqrt(v):
    return lax.rsqrt(jnp.where(v > 0.0, v, 1.0))


def kernel(count_all, snps, geno, annot, first_h, last_h, out,
           x_v, l0, r1, a_own, a_prev, a_next,
           s1, s2, s3, f1, f2, f3, c1, c2, c3, k1, k2, k3, g1, g2, g3, o1, o2, o3, score_v, folded_v, ss_own, ss_all, ss_tot, ss_side,
           p1, p2, p3, t1, t2, t3,
           first, last, win_sem, x_sem, a_sem, halo_send, halo_recv, ring,
           ss_send, ss_recv, side_send, side_recv,
           c_send, c_recv, g_send, g_recv, t_send, t_recv1, t_recv2, t_recv3):
    s = lax.axis_index("snp")
    z = lax.axis_index("ind")
    ns, nz = snps, 16
    right, left = lax.rem(s + 1, ns), lax.rem(s + ns - 1, ns)

    def zpeer(d):
        return lax.rem(z + d + nz, nz)

    def rcopy(src, dst, ssem, rsem, dev):
        return pltpu.make_async_remote_copy(
            src_ref=src, dst_ref=dst, send_sem=ssem, recv_sem=rsem,
            device_id=dev, device_id_type=MESH)

    def signal(sem, dev):
        pl.semaphore_signal(sem, inc=1, device_id=dev, device_id_type=MESH)

    x_copy = pltpu.make_async_copy(geno, x_v, x_sem)
    x_copy.start()
    a_copy = pltpu.make_async_copy(annot, a_own, a_sem)
    a_copy.start()
    f_copy = pltpu.make_async_copy(first_h, first, win_sem.at[0])
    e_copy = pltpu.make_async_copy(last_h, last, win_sem.at[1])
    f_copy.start()
    e_copy.start()

    barrier = pltpu.get_barrier_semaphore()
    signal(barrier, {"snp": left})
    signal(barrier, {"snp": right})
    signal(barrier, {"ind": zpeer(1)})
    signal(barrier, {"ind": zpeer(-1)})
    pl.semaphore_wait(barrier, 4)

    h_left = rcopy(geno.at[:, pl.ds(0, 256)], l0, halo_send.at[0], halo_recv.at[0], {"snp": left})
    h_right = rcopy(geno.at[:, pl.ds(256, 256)], r1, halo_send.at[1], halo_recv.at[1], {"snp": right})
    h_left.start()
    h_right.start()
    ann_l = rcopy(annot, a_next, halo_send.at[2], halo_recv.at[2], {"snp": left})
    ann_r = rcopy(annot, a_prev, halo_send.at[3], halo_recv.at[3], {"snp": right})
    ann_l.start()
    ann_r.start()

    signal(ring.at[0], {"ind": zpeer(1)})
    signal(ring.at[0], {"ind": zpeer(-1)})

    eye = (lax.broadcasted_iota(jnp.int32, (256, 256), 0)
           == lax.broadcasted_iota(jnp.int32, (256, 256), 1))

    def ss_copy(d):
        dest = lax.rem(z + d, nz)
        return rcopy(ss_own, ss_all.at[z], ss_send.at[d], ss_recv.at[z], {"ind": dest})

    def each_peer(body, lo=1, hi=16):
        def step(d, carry):
            body(d)
            return carry
        lax.fori_loop(lo, hi, step, 0)

    def span(lo, hi, body, top=16):
        def step(t, carry):
            @pl.when((t >= lo) & (t < hi))
            def _():
                body(t)
            return carry
        lax.fori_loop(0, top, step, 0)

    def eight(first_e, body, end_e=8):
        def step(e, carry):
            body(e)
            return carry
        lax.fori_loop(first_e, end_e, step, 0)

    even_z = lax.rem(z, 2) == 0
    toward = (jnp.where(even_z, 1, -1), jnp.where(even_z, -1, 1), jnp.where(even_z, -1, 1))
    lows = (0, 0, 8)

    def pieces(k, t, act):
        if k == 0:
            cases = [((t // 4) == g, g, 4 - g) for g in range(4)]
        elif k == 1:
            cases = [(t < 4, 0, 1), (t >= 4, 0, 2)]
        else:
            cases = [((t >= 8) & (t < 12), 0, 2), (t >= 12, 1, 1)]
        for hit, start, size in cases:
            @pl.when(hit)
            def _(start=start, size=size):
                act(pl.ds(start, size))

    sends, wides, gives, sums, ends, owns = (s1, s2, s3), (f1, f2, f3), (c1, c2, c3), (k1, k2, k3), (g1, g2, g3), (o1, o2, o3)

    def give_copy(k, t, part):
        i = t - lows[k]
        return rcopy(sends[k].at[i, part], gives[k].at[i, part], c_send.at[k, t], c_recv.at[k, t],
                     {"ind": zpeer(toward[k])})

    def give(k):
        def body(n):
            t = zpeer(toward[k] * (8 - n))
            pieces(k, t, lambda part: give_copy(k, t, part).start())
        eight(0, body)

    def give_wait(k):
        def body(e):
            t = zpeer(toward[k] * (e + 1))
            pieces(k, t, lambda part: give_copy(k, t, part).wait_send())
        eight(0, body)

    def end_copy(k, e, t, part):
        return rcopy(sums[k].at[t - lows[k], part], ends[k].at[e, part], g_send.at[k, e], g_recv.at[k, e], {"ind": t})

    def combine(k, near=0, far=8):
        def body(n):
            e = near + far - 1 - n
            t = zpeer(-toward[k] * e)
            i = t - lows[k]
            pieces(k, t, lambda part: give_copy(k, t, part).wait_recv())

            def add():
                total = wides[k][i] + gives[k][i].astype(F32)

                @pl.when(e == 0)
                def _():
                    owns[k][...] = total

                @pl.when(e > 0)
                def _():
                    sums[k][i] = total.astype(BF16)
            if lows[k]:
                pl.when(t >= lows[k])(add)
            else:
                add()

            def go():
                pieces(k, t, lambda part: end_copy(k, e, t, part).start())
            pl.when(e > 0)(go)

        eight(near, body, far)

    def end_send_wait(k):
        def body(e):
            t = zpeer(-toward[k] * e)
            pieces(k, t, lambda part: end_copy(k, e, t, part).wait_send())
        eight(1, body)

    def end_recv_wait(k):
        def body(e):
            pieces(k, z, lambda part: rcopy(
                ends[k].at[e, part], ends[k].at[e, part], g_send.at[k, e], g_recv.at[k, e],
                {"ind": zpeer(toward[k])}).wait_recv())
        eight(1, body)

    def keep_blocks(k, gram, rows_at, block_at):
        n = gram.shape[0] // 32
        for b in range(gram.shape[1] // 128):
            tile = gram[:, 128 * b:128 * b + 128].reshape(n, 32, 128)
            wides[k][rows_at:rows_at + n, block_at + b] = tile
            sends[k][rows_at:rows_at + n, block_at + b] = tile.astype(BF16)

    def next_part():
        h_left.wait_recv()
        keep_blocks(1, tdot(x_v[...], l0[...]), 0, 0)
        give(1)

    def prev_part():
        h_right.wait_recv()
        keep_blocks(2, tdot(x_v[:, 256:512], r1[...]), 0, 0)
        give(2)

    odd = lax.rem(s, 2) == 1

    def either(if_odd, if_even):
        pl.when(odd)(if_odd)
        pl.when(jnp.logical_not(odd))(if_even)

    pl.semaphore_wait(ring.at[0], 2)
    signal(ring.at[1], {"ind": zpeer(2)})
    signal(ring.at[1], {"ind": zpeer(-2)})
    x_copy.wait()
    m_lo = tdot(x_v[:, 0:256], x_v[...])
    keep_blocks(0, m_lo, 0, 0)
    ss_own[:, 0:256] = jnp.sum(jnp.where(eye, m_lo[:, 0:256], 0.0), axis=0, keepdims=True)
    pl.semaphore_wait(ring.at[1], 2)
    signal(ring.at[2], {"ind": zpeer(4)})
    signal(ring.at[2], {"ind": zpeer(-4)})
    m_hi = tdot(x_v[:, 256:512], x_v[:, 256:512])
    keep_blocks(0, m_hi, 8, 2)
    give(0)
    ss_own[:, 256:512] = jnp.sum(jnp.where(eye, m_hi, 0.0), axis=0, keepdims=True)
    each_peer(lambda d: ss_copy(d).start(), 1, 5)
    each_peer(lambda d: ss_copy(d).start(), 12, 16)
    either(prev_part, next_part)
    pl.semaphore_wait(ring.at[2], 2)
    each_peer(lambda d: ss_copy(d).start(), 5, 12)
    combine(0)
    either(lambda: combine(2), lambda: combine(1))
    either(next_part, prev_part)

    ss_all[z] = ss_own[...]

    def ss_wait(d):
        origin = lax.rem(z + d, nz)
        rcopy(ss_own, ss_all.at[origin], ss_send.at[d], ss_recv.at[origin], {"ind": origin}).wait_recv()
    each_peer(ss_wait)
    ss_tot[...] = jnp.sum(ss_all[...], axis=0)
    side_l = rcopy(ss_tot, ss_side.at[1], side_send.at[0], side_recv.at[1], {"snp": left})
    side_r = rcopy(ss_tot, ss_side.at[0], side_send.at[1], side_recv.at[0], {"snp": right})
    side_l.start()
    side_r.start()
    either(lambda: combine(1), lambda: combine(2))

    def column(row, offset):
        n = row.shape[1]
        hit = (lax.broadcasted_iota(jnp.int32, (32, n), 1)
               == lax.broadcasted_iota(jnp.int32, (32, n), 0) + offset)
        return jnp.sum(jnp.where(hit, jnp.broadcast_to(row, (32, n)), jnp.zeros((), row.dtype)),
                       axis=1, keepdims=True)

    lead = z * 32
    f_copy.wait()
    e_copy.wait()
    low = column(first[...], 0)
    high = column(last[...], 0)
    row_scale = safe_rsqrt(column(ss_tot[...], lead))

    def weigh(gram, col_ss, col_first, keep):
        n = gram.shape[1]
        corr = gram * row_scale * safe_rsqrt(col_ss)
        squared = corr * corr
        adjusted = squared - (1.0 - squared) / (count_all - 2.0)
        ids = lax.broadcasted_iota(jnp.int32, (32, n), 1) + col_first
        inside = (ids >= low) & (ids < high) & keep
        return jnp.where(inside, adjusted, 0.0).astype(BF16).astype(F32)

    def summed(k, width):
        total = owns[k][...]
        for e in range(1, 8):
            total = total + ends[k][e].astype(F32)
        return jnp.concatenate([total[b] for b in range(width)], axis=1)

    lane = lax.broadcasted_iota(jnp.int32, (8, 128), 1) // 32

    def pack(weights, buf):
        for b in range(weights.shape[1] // 128):
            for u in range(4):
                tile = jnp.zeros((8, 128), F32)
                for v in range(4):
                    piece = weights[8 * v:8 * v + 8, 128 * b:128 * b + 128]
                    shift = (32 * (v - u)) % 128
                    if shift:
                        piece = pltpu.roll(piece, shift, 1)
                    tile = jnp.where(lane == v, piece, tile)
                buf[4 * b + u] = tile.astype(BF16)

    rows = lax.broadcasted_iota(jnp.int32, (32, 1), 0) + lead

    def cols(n):
        return lax.broadcasted_iota(jnp.int32, (32, n), 1)

    end_recv_wait(0)
    gram1 = jnp.where(rows == cols(512), jnp.broadcast_to(ss_tot[...], (32, 512)), summed(0, 4))
    w1 = weigh(gram1, ss_tot[...], s * 512, cols(512) >= lead)
    pack(w1, p1)

    def t1_copy(t):
        return rcopy(p1.at[t], t1.at[z], t_send.at[0, t], t_recv1.at[z], {"ind": t})

    span(z + 1, nz, lambda t: t1_copy(t).start())

    side_l.wait_send()
    side_r.wait_send()
    side_l.wait_recv()
    side_r.wait_recv()
    def t2_copy(t):
        return rcopy(p2.at[t], t2.at[z], t_send.at[1, t], t_recv2.at[z], {"snp": right, "ind": t})

    def t3_copy(t):
        return rcopy(p3.at[t - 8], t3.at[z - 8], t_send.at[2, t], t_recv3.at[z - 8], {"snp": left, "ind": t})

    t3_first = jnp.where(z >= 8, z, nz)
    a_copy.wait()
    ann_l.wait_recv()
    ann_r.wait_recv()
    score_v[...] = mm(w1.astype(BF16), a_own[...])

    def next_own():
        end_recv_wait(1)
        w2 = weigh(summed(1, 2), ss_side[1][:, 0:256], (s + 1) * 512, cols(256) <= rows)
        pack(w2, p2)
        span(0, jnp.minimum(z + 1, 8), lambda t: t2_copy(t).start())
        score_v[...] += mm(w2.astype(BF16), a_next[0:256, :])

    def prev_own():
        end_recv_wait(2)
        w3 = weigh(summed(2, 2), ss_side[0][:, 256:512], s * 512 - 256, (cols(256) + 256 >= rows) & (z >= 8))
        pack(w3, p3)
        span(t3_first, nz, lambda t: t3_copy(t).start())
        score_v[...] += mm(w3.astype(BF16), a_prev[256:512, :])

    either(prev_own, next_own)
    either(next_own, prev_own)

    h_left.wait_send()
    h_right.wait_send()
    ann_l.wait_send()
    ann_r.wait_send()
    each_peer(lambda d: ss_copy(d).wait_send())
    for k in range(3):
        give_wait(k)
        end_send_wait(k)
    span(z + 1, nz, lambda t: t1_copy(t).wait_send())
    span(0, jnp.minimum(z + 1, 8), lambda t: t2_copy(t).wait_send())
    span(t3_first, nz, lambda t: t3_copy(t).wait_send())

    def t_recv_wait(buf, sems, base, i):
        rcopy(buf.at[i - base], buf.at[i - base], t_send.at[0, i], sems.at[i - base], {"ind": i}).wait_recv()

    def spread(buf, lo, hi, base):
        n = buf.shape[0]
        shape = (n, 4, 8, 128)
        tiles = jnp.broadcast_to(buf[...].astype(F32).reshape(n, 1, 8, 128), shape)
        src = lax.broadcasted_iota(jnp.int32, shape, 0) + base
        v = lax.broadcasted_iota(jnp.int32, shape, 1)
        ln = lax.broadcasted_iota(jnp.int32, shape, 3) // 32
        keep = (ln == v) & (src >= lo) & (src < hi)
        return jnp.where(keep, tiles, 0.0).reshape(n * 32, 128).astype(BF16)

    span(0, z, lambda i: t_recv_wait(t1, t_recv1, 0, i))
    folded = tdot(spread(t1, 0, z, 0), a_own[...])
    folded_v[...] = folded
    span(jnp.where(z < 8, z, nz), nz, lambda i: t_recv_wait(t2, t_recv2, 0, i))
    span(8, jnp.where(z >= 8, z + 1, 0), lambda i: t_recv_wait(t3, t_recv3, 8, i))
    score = score_v[...]
    folded = folded_v[...]
    folded = folded + tdot(spread(t2, jnp.where(z < 8, z, nz), nz, 0), a_prev[...])
    folded = folded + tdot(spread(t3, 8, jnp.where(z >= 8, z + 1, 0), 8), a_next[256:512, :])
    for v in range(4):
        score = score + folded[32 * v:32 * v + 32, :]
    out[...] = score


def per_device(count_all, snps, genotypes, annotations, window_start, window_end):
    dma = pltpu.SemaphoreType.DMA
    vm = pltpu.VMEM
    any_spec = pl.BlockSpec(memory_space=pltpu.HBM)
    vmem_spec = pl.BlockSpec(memory_space=pltpu.VMEM)
    return pl.pallas_call(
        functools.partial(kernel, count_all, snps),
        out_shape=jax.ShapeDtypeStruct((32, 512), F32),
        in_specs=[any_spec, any_spec, any_spec, any_spec],
        out_specs=vmem_spec,
        scratch_shapes=[
            vm((2048, 512), BF16), vm((2048, 256), BF16), vm((2048, 256), BF16),
            vm((512, 512), BF16), vm((512, 512), BF16), vm((512, 512), BF16),
            *[vm((n, b, 32, 128), kind) for kind in (BF16, F32, BF16, BF16) for n, b in ((16, 4), (16, 2), (8, 2))],
            *[vm((8, b, 32, 128), BF16) for b in (4, 2, 2)],
            *[vm((b, 32, 128), F32) for b in (4, 2, 2)], vm((32, 512), F32), vm((128, 512), F32),
            vm((1, 512), F32), vm((16, 1, 512), F32), vm((1, 512), F32), vm((2, 1, 512), F32),
            vm((16, 8, 128), BF16), vm((8, 8, 128), BF16), vm((8, 8, 128), BF16),
            vm((16, 8, 128), BF16), vm((16, 8, 128), BF16), vm((8, 8, 128), BF16),
            vm((1, 32), jnp.int32), vm((1, 32), jnp.int32), dma((2,)),
            dma, dma, dma((4,)), dma((4,)), pltpu.SemaphoreType.REGULAR((3,)),
            dma((16,)), dma((16,)), dma((2,)), dma((2,)),
            dma((3, 16)), dma((3, 16)), dma((3, 8)), dma((3, 8)),
            dma((3, 16)), dma((16,)), dma((16,)), dma((8,)),
        ],
        compiler_params=pltpu.CompilerParams(
            collective_id=0, has_side_effects=True, vmem_limit_bytes=67043328),
        name="ld_scores",
    )(genotypes, annotations, window_start.reshape(1, 32), window_end.reshape(1, 32))


def solution(mesh):
    snps, groups = mesh.shape["snp"], mesh.shape["ind"]
    body = functools.partial(per_device, float(2048 * groups), snps)
    in_specs = (P("ind", "snp"), P("snp", None), P(("snp", "ind")), P(("snp", "ind")))
    return jax.shard_map(
        body, mesh=mesh, in_specs=in_specs, out_specs=P(("snp", "ind"), None), check_vma=False)
```

```python
import functools

import jax
import jax.numpy as jnp
from jax import lax
from jax.experimental import pallas as pl
from jax.experimental.pallas import tpu as pltpu
from jax.sharding import PartitionSpec as P

MESH = pl.DeviceIdType.MESH
BF16, F32 = jnp.bfloat16, jnp.float32


def tdot(left, right):
    return lax.dot_general(left, right, (((0,), (0,)), ((), ())), preferred_element_type=F32)


def mm(left, right):
    return jnp.dot(left, right, preferred_element_type=F32)


def safe_rsqrt(v):
    return lax.rsqrt(jnp.where(v > 0.0, v, 1.0))


def kernel(count_all, snps, geno, annot, first_h, last_h, out,
           x_v, l0, r1, a_own, a_prev, a_next,
           s1, s2, s3, f1, f2, f3, c1, c2, c3, k1, k2, k3, g1, g2, g3, o1, o2, o3, score_v, folded_v, ss_own, ss_all, ss_tot, ss_side,
           p1, p2, p3, t1, t2, t3,
           first, last, win_sem, x_sem, a_sem, halo_send, halo_recv, ring,
           ss_send, ss_recv, side_send, side_recv,
           c_send, c_recv, g_send, g_recv, t_send, t_recv1, t_recv2, t_recv3):
    s = lax.axis_index("snp")
    z = lax.axis_index("ind")
    ns, nz = snps, 16
    right, left = lax.rem(s + 1, ns), lax.rem(s + ns - 1, ns)

    def zpeer(d):
        return lax.rem(z + d + nz, nz)

    def rcopy(src, dst, ssem, rsem, dev):
        return pltpu.make_async_remote_copy(
            src_ref=src, dst_ref=dst, send_sem=ssem, recv_sem=rsem,
            device_id=dev, device_id_type=MESH)

    def signal(sem, dev):
        pl.semaphore_signal(sem, inc=1, device_id=dev, device_id_type=MESH)

    x_copy = pltpu.make_async_copy(geno, x_v, x_sem)
    x_copy.start()
    a_copy = pltpu.make_async_copy(annot, a_own, a_sem)
    a_copy.start()
    f_copy = pltpu.make_async_copy(first_h, first, win_sem.at[0])
    e_copy = pltpu.make_async_copy(last_h, last, win_sem.at[1])
    f_copy.start()
    e_copy.start()

    barrier = pltpu.get_barrier_semaphore()
    signal(barrier, {"snp": left})
    signal(barrier, {"snp": right})
    signal(barrier, {"ind": zpeer(1)})
    signal(barrier, {"ind": zpeer(-1)})
    pl.semaphore_wait(barrier, 4)

    h_left = rcopy(geno.at[:, pl.ds(0, 256)], l0, halo_send.at[0], halo_recv.at[0], {"snp": left})
    h_right = rcopy(geno.at[:, pl.ds(256, 256)], r1, halo_send.at[1], halo_recv.at[1], {"snp": right})
    h_left.start()
    h_right.start()
    ann_l = rcopy(annot, a_next, halo_send.at[2], halo_recv.at[2], {"snp": left})
    ann_r = rcopy(annot, a_prev, halo_send.at[3], halo_recv.at[3], {"snp": right})
    ann_l.start()
    ann_r.start()

    signal(ring.at[0], {"ind": zpeer(1)})
    signal(ring.at[0], {"ind": zpeer(-1)})

    eye = (lax.broadcasted_iota(jnp.int32, (256, 256), 0)
           == lax.broadcasted_iota(jnp.int32, (256, 256), 1))

    def ss_copy(d):
        dest = lax.rem(z + d, nz)
        return rcopy(ss_own, ss_all.at[z], ss_send.at[d], ss_recv.at[z], {"ind": dest})

    def each_peer(body, lo=1, hi=16):
        def step(d, carry):
            body(d)
            return carry
        lax.fori_loop(lo, hi, step, 0)

    def span(lo, hi, body, top=16):
        def step(t, carry):
            @pl.when((t >= lo) & (t < hi))
            def _():
                body(t)
            return carry
        lax.fori_loop(0, top, step, 0)

    def eight(first_e, body, end_e=8):
        def step(e, carry):
            body(e)
            return carry
        lax.fori_loop(first_e, end_e, step, 0)

    even_z = lax.rem(z, 2) == 0
    toward = (jnp.where(even_z, 1, -1), jnp.where(even_z, -1, 1), jnp.where(even_z, -1, 1))
    lows = (0, 0, 8)

    def pieces(k, t, act):
        if k == 0:
            cases = [((t // 4) == g, g, 4 - g) for g in range(4)]
        elif k == 1:
            cases = [(t < 4, 0, 1), (t >= 4, 0, 2)]
        else:
            cases = [((t >= 8) & (t < 12), 0, 2), (t >= 12, 1, 1)]
        for hit, start, size in cases:
            @pl.when(hit)
            def _(start=start, size=size):
                act(pl.ds(start, size))

    sends, wides, gives, sums, ends, owns = (s1, s2, s3), (f1, f2, f3), (c1, c2, c3), (k1, k2, k3), (g1, g2, g3), (o1, o2, o3)

    def give_copy(k, t, part):
        i = t - lows[k]
        return rcopy(sends[k].at[i, part], gives[k].at[i, part], c_send.at[k, t], c_recv.at[k, t],
                     {"ind": zpeer(toward[k])})

    def give(k, lo=0, hi=16):
        def body(n):
            t = zpeer(toward[k] * (8 - n))

            @pl.when((t >= lo) & (t < hi))
            def _():
                pieces(k, t, lambda part: give_copy(k, t, part).start())
        eight(0, body)

    def give_wait(k):
        def body(e):
            t = zpeer(toward[k] * (e + 1))
            pieces(k, t, lambda part: give_copy(k, t, part).wait_send())
        eight(0, body)

    def end_copy(k, e, t, part):
        return rcopy(sums[k].at[t - lows[k], part], ends[k].at[e, part], g_send.at[k, e], g_recv.at[k, e], {"ind": t})

    def combine(k, near=0, far=8):
        def body(n):
            e = near + far - 1 - n
            t = zpeer(-toward[k] * e)
            i = t - lows[k]
            pieces(k, t, lambda part: give_copy(k, t, part).wait_recv())

            def add():
                total = wides[k][i] + gives[k][i].astype(F32)

                @pl.when(e == 0)
                def _():
                    owns[k][...] = total

                @pl.when(e > 0)
                def _():
                    sums[k][i] = total.astype(BF16)
            if lows[k]:
                pl.when(t >= lows[k])(add)
            else:
                add()

            def go():
                pieces(k, t, lambda part: end_copy(k, e, t, part).start())
            pl.when(e > 0)(go)

        eight(near, body, far)

    def end_send_wait(k):
        def body(e):
            t = zpeer(-toward[k] * e)
            pieces(k, t, lambda part: end_copy(k, e, t, part).wait_send())
        eight(1, body)

    def end_recv_wait(k):
        def body(e):
            pieces(k, z, lambda part: rcopy(
                ends[k].at[e, part], ends[k].at[e, part], g_send.at[k, e], g_recv.at[k, e],
                {"ind": zpeer(toward[k])}).wait_recv())
        eight(1, body)

    def keep_blocks(k, gram, rows_at, block_at):
        n = gram.shape[0] // 32
        for b in range(gram.shape[1] // 128):
            tile = gram[:, 128 * b:128 * b + 128].reshape(n, 32, 128)
            wides[k][rows_at:rows_at + n, block_at + b] = tile
            sends[k][rows_at:rows_at + n, block_at + b] = tile.astype(BF16)

    def next_part():
        h_left.wait_recv()
        keep_blocks(1, tdot(x_v[...], l0[...]), 0, 0)
        give(1)

    def prev_part():
        h_right.wait_recv()
        keep_blocks(2, tdot(x_v[:, 256:512], r1[...]), 0, 0)
        give(2)

    odd = lax.rem(s, 2) == 1

    def either(if_odd, if_even):
        pl.when(odd)(if_odd)
        pl.when(jnp.logical_not(odd))(if_even)

    pl.semaphore_wait(ring.at[0], 2)
    signal(ring.at[1], {"ind": zpeer(2)})
    signal(ring.at[1], {"ind": zpeer(-2)})
    x_copy.wait()
    m_lo = tdot(x_v[:, 0:256], x_v[...])
    keep_blocks(0, m_lo, 0, 0)
    give(0, 0, 8)
    ss_own[:, 0:256] = jnp.sum(jnp.where(eye, m_lo[:, 0:256], 0.0), axis=0, keepdims=True)
    pl.semaphore_wait(ring.at[1], 2)
    signal(ring.at[2], {"ind": zpeer(4)})
    signal(ring.at[2], {"ind": zpeer(-4)})
    m_hi = tdot(x_v[:, 256:512], x_v[:, 256:512])
    keep_blocks(0, m_hi, 8, 2)
    give(0, 8, 16)
    ss_own[:, 256:512] = jnp.sum(jnp.where(eye, m_hi, 0.0), axis=0, keepdims=True)
    each_peer(lambda d: ss_copy(d).start(), 1, 5)
    each_peer(lambda d: ss_copy(d).start(), 12, 16)
    either(prev_part, next_part)
    pl.semaphore_wait(ring.at[2], 2)
    each_peer(lambda d: ss_copy(d).start(), 5, 12)
    combine(0)
    either(lambda: combine(2), lambda: combine(1))
    either(next_part, prev_part)

    ss_all[z] = ss_own[...]

    def ss_wait(d):
        origin = lax.rem(z + d, nz)
        rcopy(ss_own, ss_all.at[origin], ss_send.at[d], ss_recv.at[origin], {"ind": origin}).wait_recv()
    each_peer(ss_wait)
    ss_tot[...] = jnp.sum(ss_all[...], axis=0)
    side_l = rcopy(ss_tot, ss_side.at[1], side_send.at[0], side_recv.at[1], {"snp": left})
    side_r = rcopy(ss_tot, ss_side.at[0], side_send.at[1], side_recv.at[0], {"snp": right})
    side_l.start()
    side_r.start()
    either(lambda: combine(1), lambda: combine(2))

    def column(row, offset):
        n = row.shape[1]
        hit = (lax.broadcasted_iota(jnp.int32, (32, n), 1)
               == lax.broadcasted_iota(jnp.int32, (32, n), 0) + offset)
        return jnp.sum(jnp.where(hit, jnp.broadcast_to(row, (32, n)), jnp.zeros((), row.dtype)),
                       axis=1, keepdims=True)

    lead = z * 32
    f_copy.wait()
    e_copy.wait()
    low = column(first[...], 0)
    high = column(last[...], 0)
    row_scale = safe_rsqrt(column(ss_tot[...], lead))

    def weigh(gram, col_ss, col_first, keep):
        n = gram.shape[1]
        corr = gram * row_scale * safe_rsqrt(col_ss)
        squared = corr * corr
        adjusted = squared - (1.0 - squared) / (count_all - 2.0)
        ids = lax.broadcasted_iota(jnp.int32, (32, n), 1) + col_first
        inside = (ids >= low) & (ids < high) & keep
        return jnp.where(inside, adjusted, 0.0).astype(BF16).astype(F32)

    def summed(k, width):
        total = owns[k][...]
        for e in range(1, 8):
            total = total + ends[k][e].astype(F32)
        return jnp.concatenate([total[b] for b in range(width)], axis=1)

    lane = lax.broadcasted_iota(jnp.int32, (8, 128), 1) // 32

    def pack(weights, buf):
        for b in range(weights.shape[1] // 128):
            for u in range(4):
                tile = jnp.zeros((8, 128), F32)
                for v in range(4):
                    piece = weights[8 * v:8 * v + 8, 128 * b:128 * b + 128]
                    shift = (32 * (v - u)) % 128
                    if shift:
                        piece = pltpu.roll(piece, shift, 1)
                    tile = jnp.where(lane == v, piece, tile)
                buf[4 * b + u] = tile.astype(BF16)

    rows = lax.broadcasted_iota(jnp.int32, (32, 1), 0) + lead

    def cols(n):
        return lax.broadcasted_iota(jnp.int32, (32, n), 1)

    end_recv_wait(0)
    gram1 = jnp.where(rows == cols(512), jnp.broadcast_to(ss_tot[...], (32, 512)), summed(0, 4))
    w1 = weigh(gram1, ss_tot[...], s * 512, cols(512) >= lead)
    pack(w1, p1)

    def t1_copy(t):
        return rcopy(p1.at[t], t1.at[z], t_send.at[0, t], t_recv1.at[z], {"ind": t})

    span(z + 1, nz, lambda t: t1_copy(t).start())

    side_l.wait_send()
    side_r.wait_send()
    side_l.wait_recv()
    side_r.wait_recv()
    def t2_copy(t):
        return rcopy(p2.at[t], t2.at[z], t_send.at[1, t], t_recv2.at[z], {"snp": right, "ind": t})

    def t3_copy(t):
        return rcopy(p3.at[t - 8], t3.at[z - 8], t_send.at[2, t], t_recv3.at[z - 8], {"snp": left, "ind": t})

    t3_first = jnp.where((z >= 8) & (s > 0), z, nz)
    t2_end = jnp.where(s < ns - 1, jnp.minimum(z + 1, 8), 0)
    t2_from = jnp.where((z < 8) & (s > 0), z, nz)
    t3_end = jnp.where((z >= 8) & (s < ns - 1), z + 1, 0)
    a_copy.wait()
    ann_l.wait_recv()
    ann_r.wait_recv()
    score_v[...] = mm(w1.astype(BF16), a_own[...])

    def next_own():
        end_recv_wait(1)
        w2 = weigh(summed(1, 2), ss_side[1][:, 0:256], (s + 1) * 512, cols(256) <= rows)
        pack(w2, p2)
        span(0, t2_end, lambda t: t2_copy(t).start())
        score_v[...] += mm(w2.astype(BF16), a_next[0:256, :])

    def prev_own():
        end_recv_wait(2)
        w3 = weigh(summed(2, 2), ss_side[0][:, 256:512], s * 512 - 256, (cols(256) + 256 >= rows) & (z >= 8))
        pack(w3, p3)
        span(t3_first, nz, lambda t: t3_copy(t).start())
        score_v[...] += mm(w3.astype(BF16), a_prev[256:512, :])

    either(prev_own, next_own)
    either(next_own, prev_own)

    h_left.wait_send()
    h_right.wait_send()
    ann_l.wait_send()
    ann_r.wait_send()
    each_peer(lambda d: ss_copy(d).wait_send())
    for k in range(3):
        give_wait(k)
        end_send_wait(k)
    span(z + 1, nz, lambda t: t1_copy(t).wait_send())
    span(0, t2_end, lambda t: t2_copy(t).wait_send())
    span(t3_first, nz, lambda t: t3_copy(t).wait_send())

    def t_recv_wait(buf, sems, base, i):
        rcopy(buf.at[i - base], buf.at[i - base], t_send.at[0, i], sems.at[i - base], {"ind": i}).wait_recv()

    def spread(buf, lo, hi, base):
        n = buf.shape[0]
        shape = (n, 4, 8, 128)
        tiles = jnp.broadcast_to(buf[...].astype(F32).reshape(n, 1, 8, 128), shape)
        src = lax.broadcasted_iota(jnp.int32, shape, 0) + base
        v = lax.broadcasted_iota(jnp.int32, shape, 1)
        ln = lax.broadcasted_iota(jnp.int32, shape, 3) // 32
        keep = (ln == v) & (src >= lo) & (src < hi)
        return jnp.where(keep, tiles, 0.0).reshape(n * 32, 128).astype(BF16)

    span(0, z, lambda i: t_recv_wait(t1, t_recv1, 0, i))
    folded = tdot(spread(t1, 0, z, 0), a_own[...])
    folded_v[...] = folded
    span(t2_from, nz, lambda i: t_recv_wait(t2, t_recv2, 0, i))
    span(8, t3_end, lambda i: t_recv_wait(t3, t_recv3, 8, i))
    score = score_v[...]
    folded = folded_v[...]
    folded = folded + tdot(spread(t2, t2_from, nz, 0), a_prev[...])
    folded = folded + tdot(spread(t3, 8, t3_end, 8), a_next[256:512, :])
    for v in range(4):
        score = score + folded[32 * v:32 * v + 32, :]
    out[...] = score


def per_device(count_all, snps, genotypes, annotations, window_start, window_end):
    dma = pltpu.SemaphoreType.DMA
    vm = pltpu.VMEM
    any_spec = pl.BlockSpec(memory_space=pltpu.HBM)
    vmem_spec = pl.BlockSpec(memory_space=pltpu.VMEM)
    return pl.pallas_call(
        functools.partial(kernel, count_all, snps),
        out_shape=jax.ShapeDtypeStruct((32, 512), F32),
        in_specs=[any_spec, any_spec, any_spec, any_spec],
        out_specs=vmem_spec,
        scratch_shapes=[
            vm((2048, 512), BF16), vm((2048, 256), BF16), vm((2048, 256), BF16),
            vm((512, 512), BF16), vm((512, 512), BF16), vm((512, 512), BF16),
            *[vm((n, b, 32, 128), kind) for kind in (BF16, F32, BF16, BF16) for n, b in ((16, 4), (16, 2), (8, 2))],
            *[vm((8, b, 32, 128), BF16) for b in (4, 2, 2)],
            *[vm((b, 32, 128), F32) for b in (4, 2, 2)], vm((32, 512), F32), vm((128, 512), F32),
            vm((1, 512), F32), vm((16, 1, 512), F32), vm((1, 512), F32), vm((2, 1, 512), F32),
            vm((16, 8, 128), BF16), vm((8, 8, 128), BF16), vm((8, 8, 128), BF16),
            vm((16, 8, 128), BF16), vm((16, 8, 128), BF16), vm((8, 8, 128), BF16),
            vm((1, 32), jnp.int32), vm((1, 32), jnp.int32), dma((2,)),
            dma, dma, dma((4,)), dma((4,)), pltpu.SemaphoreType.REGULAR((3,)),
            dma((16,)), dma((16,)), dma((2,)), dma((2,)),
            dma((3, 16)), dma((3, 16)), dma((3, 8)), dma((3, 8)),
            dma((3, 16)), dma((16,)), dma((16,)), dma((8,)),
        ],
        compiler_params=pltpu.CompilerParams(
            collective_id=0, has_side_effects=True, vmem_limit_bytes=67043328),
        name="ld_scores",
    )(genotypes, annotations, window_start.reshape(1, 32), window_end.reshape(1, 32))


def solution(mesh):
    snps, groups = mesh.shape["snp"], mesh.shape["ind"]
    body = functools.partial(per_device, float(2048 * groups), snps)
    in_specs = (P("ind", "snp"), P("snp", None), P(("snp", "ind")), P(("snp", "ind")))
    return jax.shard_map(
        body, mesh=mesh, in_specs=in_specs, out_specs=P(("snp", "ind"), None), check_vma=False)
```

```python
import functools

import jax
import jax.numpy as jnp
from jax import lax
from jax.experimental import pallas as pl
from jax.experimental.pallas import tpu as pltpu
from jax.sharding import PartitionSpec as P

MESH = pl.DeviceIdType.MESH
BF16, F32 = jnp.bfloat16, jnp.float32


def tdot(left, right):
    return lax.dot_general(left, right, (((0,), (0,)), ((), ())), preferred_element_type=F32)


def mm(left, right):
    return jnp.dot(left, right, preferred_element_type=F32)


def safe_rsqrt(v):
    return lax.rsqrt(jnp.where(v > 0.0, v, 1.0))


def kernel(count_all, snps, geno, annot, first_h, last_h, out,
           x_v, l0, r1, a_own, a_prev, a_next,
           s1, s2, s3, f1, f2, f3, c1, c2, c3, k1, k2, k3, g1, g2, g3, o1, o2, o3, score_v, folded_v, ss_own, ss_all, ss_tot, ss_side,
           p1, p2, p3, t1, t2, t3,
           first, last, win_sem, x_sem, a_sem, halo_send, halo_recv, ring,
           ss_send, ss_recv, side_send, side_recv,
           c_send, c_recv, g_send, g_recv, t_send, t_recv1, t_recv2, t_recv3):
    s = lax.axis_index("snp")
    z = lax.axis_index("ind")
    ns, nz = snps, 16
    right, left = lax.rem(s + 1, ns), lax.rem(s + ns - 1, ns)

    def zpeer(d):
        return lax.rem(z + d + nz, nz)

    def rcopy(src, dst, ssem, rsem, dev):
        return pltpu.make_async_remote_copy(
            src_ref=src, dst_ref=dst, send_sem=ssem, recv_sem=rsem,
            device_id=dev, device_id_type=MESH)

    def signal(sem, dev):
        pl.semaphore_signal(sem, inc=1, device_id=dev, device_id_type=MESH)

    x_copy = pltpu.make_async_copy(geno, x_v, x_sem)
    x_copy.start()
    a_copy = pltpu.make_async_copy(annot, a_own, a_sem)
    a_copy.start()
    f_copy = pltpu.make_async_copy(first_h, first, win_sem.at[0])
    e_copy = pltpu.make_async_copy(last_h, last, win_sem.at[1])
    f_copy.start()
    e_copy.start()

    barrier = pltpu.get_barrier_semaphore()
    signal(barrier, {"snp": left})
    signal(barrier, {"snp": right})
    signal(barrier, {"ind": zpeer(1)})
    signal(barrier, {"ind": zpeer(-1)})
    pl.semaphore_wait(barrier, 4)

    h_left = rcopy(geno.at[:, pl.ds(0, 256)], l0, halo_send.at[0], halo_recv.at[0], {"snp": left})
    h_right = rcopy(geno.at[:, pl.ds(256, 256)], r1, halo_send.at[1], halo_recv.at[1], {"snp": right})
    h_left.start()
    h_right.start()
    ann_l = rcopy(annot, a_next, halo_send.at[2], halo_recv.at[2], {"snp": left})
    ann_r = rcopy(annot, a_prev, halo_send.at[3], halo_recv.at[3], {"snp": right})
    ann_l.start()
    ann_r.start()

    signal(ring.at[0], {"ind": zpeer(1)})
    signal(ring.at[0], {"ind": zpeer(-1)})

    eye = (lax.broadcasted_iota(jnp.int32, (256, 256), 0)
           == lax.broadcasted_iota(jnp.int32, (256, 256), 1))

    def ss_copy(d):
        dest = lax.rem(z + d, nz)
        return rcopy(ss_own, ss_all.at[z], ss_send.at[d], ss_recv.at[z], {"ind": dest})

    def each_peer(body, lo=1, hi=16):
        def step(d, carry):
            body(d)
            return carry
        lax.fori_loop(lo, hi, step, 0)

    def span(lo, hi, body, top=16):
        def step(t, carry):
            @pl.when((t >= lo) & (t < hi))
            def _():
                body(t)
            return carry
        lax.fori_loop(0, top, step, 0)

    def eight(first_e, body, end_e=8):
        def step(e, carry):
            body(e)
            return carry
        lax.fori_loop(first_e, end_e, step, 0)

    even_z = lax.rem(z, 2) == 0
    toward = (jnp.where(even_z, 1, -1), jnp.where(even_z, -1, 1), jnp.where(even_z, -1, 1))
    lows = (0, 0, 8)

    def pieces(k, t, act):
        if k == 0:
            cases = [((t // 4) == g, g, 4 - g) for g in range(4)]
        elif k == 1:
            cases = [(t < 4, 0, 1), (t >= 4, 0, 2)]
        else:
            cases = [((t >= 8) & (t < 12), 0, 2), (t >= 12, 1, 1)]
        for hit, start, size in cases:
            @pl.when(hit)
            def _(start=start, size=size):
                act(pl.ds(start, size))

    sends, wides, gives, sums, ends, owns = (s1, s2, s3), (f1, f2, f3), (c1, c2, c3), (k1, k2, k3), (g1, g2, g3), (o1, o2, o3)

    def give_copy(k, t, part):
        i = t - lows[k]
        return rcopy(sends[k].at[i, part], gives[k].at[i, part], c_send.at[k, t], c_recv.at[k, t],
                     {"ind": zpeer(toward[k])})

    def give(k, lo=0, hi=16):
        def body(n):
            t = zpeer(toward[k] * (8 - n))

            @pl.when((t >= lo) & (t < hi))
            def _():
                pieces(k, t, lambda part: give_copy(k, t, part).start())
        eight(0, body)

    def give_wait(k):
        def body(e):
            t = zpeer(toward[k] * (e + 1))
            pieces(k, t, lambda part: give_copy(k, t, part).wait_send())
        eight(0, body)

    def end_copy(k, e, t, part):
        return rcopy(sums[k].at[t - lows[k], part], ends[k].at[e, part], g_send.at[k, e], g_recv.at[k, e], {"ind": t})

    def combine(k, near=0, far=8):
        def body(n):
            e = near + far - 1 - n
            t = zpeer(-toward[k] * e)
            i = t - lows[k]
            pieces(k, t, lambda part: give_copy(k, t, part).wait_recv())

            def add():
                total = wides[k][i] + gives[k][i].astype(F32)

                @pl.when(e == 0)
                def _():
                    owns[k][...] = total

                @pl.when(e > 0)
                def _():
                    sums[k][i] = total.astype(BF16)
            if lows[k]:
                pl.when(t >= lows[k])(add)
            else:
                add()

            def go():
                pieces(k, t, lambda part: end_copy(k, e, t, part).start())
            pl.when(e > 0)(go)

        eight(near, body, far)

    def end_send_wait(k):
        def body(e):
            t = zpeer(-toward[k] * e)
            pieces(k, t, lambda part: end_copy(k, e, t, part).wait_send())
        eight(1, body)

    def end_recv_wait(k):
        def body(e):
            pieces(k, z, lambda part: rcopy(
                ends[k].at[e, part], ends[k].at[e, part], g_send.at[k, e], g_recv.at[k, e],
                {"ind": zpeer(toward[k])}).wait_recv())
        eight(1, body)

    def keep_blocks(k, gram, rows_at, block_at):
        n = gram.shape[0] // 32
        for b in range(gram.shape[1] // 128):
            tile = gram[:, 128 * b:128 * b + 128].reshape(n, 32, 128)
            wides[k][rows_at:rows_at + n, block_at + b] = tile
            sends[k][rows_at:rows_at + n, block_at + b] = tile.astype(BF16)

    def next_part():
        h_left.wait_recv()
        keep_blocks(1, tdot(x_v[...], l0[...]), 0, 0)
        give(1)

    def prev_part():
        h_right.wait_recv()
        keep_blocks(2, tdot(x_v[:, 256:512], r1[...]), 0, 0)
        give(2)

    odd = lax.rem(s, 2) == 1

    def either(if_odd, if_even):
        pl.when(odd)(if_odd)
        pl.when(jnp.logical_not(odd))(if_even)

    pl.semaphore_wait(ring.at[0], 2)
    signal(ring.at[1], {"ind": zpeer(2)})
    signal(ring.at[1], {"ind": zpeer(-2)})
    x_copy.wait()
    m_lo = tdot(x_v[:, 0:256], x_v[...])
    keep_blocks(0, m_lo, 0, 0)
    give(0, 0, 8)
    ss_own[:, 0:256] = jnp.sum(jnp.where(eye, m_lo[:, 0:256], 0.0), axis=0, keepdims=True)
    pl.semaphore_wait(ring.at[1], 2)
    signal(ring.at[2], {"ind": zpeer(4)})
    signal(ring.at[2], {"ind": zpeer(-4)})
    m_hi = tdot(x_v[:, 256:512], x_v[:, 256:512])
    keep_blocks(0, m_hi, 8, 2)
    give(0, 8, 16)
    ss_own[:, 256:512] = jnp.sum(jnp.where(eye, m_hi, 0.0), axis=0, keepdims=True)
    each_peer(lambda d: ss_copy(d).start(), 1, 5)
    each_peer(lambda d: ss_copy(d).start(), 12, 16)
    either(prev_part, next_part)
    pl.semaphore_wait(ring.at[2], 2)
    each_peer(lambda d: ss_copy(d).start(), 5, 12)
    combine(0)
    either(lambda: combine(2), lambda: combine(1))
    has_next, has_prev = s < ns - 1, s > 0

    def where_next(body):
        pl.when(has_next)(body)

    def where_prev(body):
        pl.when(has_prev)(body)

    either(lambda: where_next(next_part), lambda: where_prev(prev_part))

    ss_all[z] = ss_own[...]

    def ss_wait(d):
        origin = lax.rem(z + d, nz)
        rcopy(ss_own, ss_all.at[origin], ss_send.at[d], ss_recv.at[origin], {"ind": origin}).wait_recv()
    each_peer(ss_wait)
    ss_tot[...] = jnp.sum(ss_all[...], axis=0)
    side_l = rcopy(ss_tot, ss_side.at[1], side_send.at[0], side_recv.at[1], {"snp": left})
    side_r = rcopy(ss_tot, ss_side.at[0], side_send.at[1], side_recv.at[0], {"snp": right})
    side_l.start()
    side_r.start()
    either(lambda: where_next(lambda: combine(1)), lambda: where_prev(lambda: combine(2)))

    def column(row, offset):
        n = row.shape[1]
        hit = (lax.broadcasted_iota(jnp.int32, (32, n), 1)
               == lax.broadcasted_iota(jnp.int32, (32, n), 0) + offset)
        return jnp.sum(jnp.where(hit, jnp.broadcast_to(row, (32, n)), jnp.zeros((), row.dtype)),
                       axis=1, keepdims=True)

    lead = z * 32
    f_copy.wait()
    e_copy.wait()
    low = column(first[...], 0)
    high = column(last[...], 0)
    row_scale = safe_rsqrt(column(ss_tot[...], lead))

    def weigh(gram, col_ss, col_first, keep):
        n = gram.shape[1]
        corr = gram * row_scale * safe_rsqrt(col_ss)
        squared = corr * corr
        adjusted = squared - (1.0 - squared) / (count_all - 2.0)
        ids = lax.broadcasted_iota(jnp.int32, (32, n), 1) + col_first
        inside = (ids >= low) & (ids < high) & keep
        return jnp.where(inside, adjusted, 0.0).astype(BF16).astype(F32)

    def summed(k, width):
        total = owns[k][...]
        for e in range(1, 8):
            total = total + ends[k][e].astype(F32)
        return jnp.concatenate([total[b] for b in range(width)], axis=1)

    lane = lax.broadcasted_iota(jnp.int32, (8, 128), 1) // 32

    def pack(weights, buf):
        for b in range(weights.shape[1] // 128):
            for u in range(4):
                tile = jnp.zeros((8, 128), F32)
                for v in range(4):
                    piece = weights[8 * v:8 * v + 8, 128 * b:128 * b + 128]
                    shift = (32 * (v - u)) % 128
                    if shift:
                        piece = pltpu.roll(piece, shift, 1)
                    tile = jnp.where(lane == v, piece, tile)
                buf[4 * b + u] = tile.astype(BF16)

    rows = lax.broadcasted_iota(jnp.int32, (32, 1), 0) + lead

    def cols(n):
        return lax.broadcasted_iota(jnp.int32, (32, n), 1)

    end_recv_wait(0)
    gram1 = jnp.where(rows == cols(512), jnp.broadcast_to(ss_tot[...], (32, 512)), summed(0, 4))
    w1 = weigh(gram1, ss_tot[...], s * 512, cols(512) >= lead)
    pack(w1, p1)

    def t1_copy(t):
        return rcopy(p1.at[t], t1.at[z], t_send.at[0, t], t_recv1.at[z], {"ind": t})

    span(z + 1, nz, lambda t: t1_copy(t).start())

    side_l.wait_send()
    side_r.wait_send()
    side_l.wait_recv()
    side_r.wait_recv()
    def t2_copy(t):
        return rcopy(p2.at[t], t2.at[z], t_send.at[1, t], t_recv2.at[z], {"snp": right, "ind": t})

    def t3_copy(t):
        return rcopy(p3.at[t - 8], t3.at[z - 8], t_send.at[2, t], t_recv3.at[z - 8], {"snp": left, "ind": t})

    t3_first = jnp.where((z >= 8) & (s > 0), z, nz)
    t2_end = jnp.where(s < ns - 1, jnp.minimum(z + 1, 8), 0)
    t2_from = jnp.where((z < 8) & (s > 0), z, nz)
    t3_end = jnp.where((z >= 8) & (s < ns - 1), z + 1, 0)
    a_copy.wait()
    ann_l.wait_recv()
    ann_r.wait_recv()
    score_v[...] = mm(w1.astype(BF16), a_own[...])

    def next_own():
        end_recv_wait(1)
        w2 = weigh(summed(1, 2), ss_side[1][:, 0:256], (s + 1) * 512, cols(256) <= rows)
        pack(w2, p2)
        span(0, t2_end, lambda t: t2_copy(t).start())
        score_v[...] += mm(w2.astype(BF16), a_next[0:256, :])

    def prev_own():
        end_recv_wait(2)
        w3 = weigh(summed(2, 2), ss_side[0][:, 256:512], s * 512 - 256, (cols(256) + 256 >= rows) & (z >= 8))
        pack(w3, p3)
        span(t3_first, nz, lambda t: t3_copy(t).start())
        score_v[...] += mm(w3.astype(BF16), a_prev[256:512, :])

    either(prev_own, next_own)
    either(lambda: where_next(next_own), lambda: where_prev(prev_own))

    h_left.wait_send()
    h_right.wait_send()
    ann_l.wait_send()
    ann_r.wait_send()
    each_peer(lambda d: ss_copy(d).wait_send())
    def part_left(k):
        give_wait(k)
        end_send_wait(k)
    part_left(0)
    where_next(lambda: part_left(1))
    where_prev(lambda: part_left(2))
    pl.when(jnp.logical_not(has_next))(h_left.wait_recv)
    pl.when(jnp.logical_not(has_prev))(h_right.wait_recv)
    span(z + 1, nz, lambda t: t1_copy(t).wait_send())
    span(0, t2_end, lambda t: t2_copy(t).wait_send())
    span(t3_first, nz, lambda t: t3_copy(t).wait_send())

    def t_recv_wait(buf, sems, base, i):
        rcopy(buf.at[i - base], buf.at[i - base], t_send.at[0, i], sems.at[i - base], {"ind": i}).wait_recv()

    def spread(buf, lo, hi, base):
        n = buf.shape[0]
        shape = (n, 4, 8, 128)
        tiles = jnp.broadcast_to(buf[...].astype(F32).reshape(n, 1, 8, 128), shape)
        src = lax.broadcasted_iota(jnp.int32, shape, 0) + base
        v = lax.broadcasted_iota(jnp.int32, shape, 1)
        ln = lax.broadcasted_iota(jnp.int32, shape, 3) // 32
        keep = (ln == v) & (src >= lo) & (src < hi)
        return jnp.where(keep, tiles, 0.0).reshape(n * 32, 128).astype(BF16)

    span(0, z, lambda i: t_recv_wait(t1, t_recv1, 0, i))
    folded = tdot(spread(t1, 0, z, 0), a_own[...])
    folded_v[...] = folded
    span(t2_from, nz, lambda i: t_recv_wait(t2, t_recv2, 0, i))
    span(8, t3_end, lambda i: t_recv_wait(t3, t_recv3, 8, i))
    score = score_v[...]
    folded = folded_v[...]
    folded = folded + tdot(spread(t2, t2_from, nz, 0), a_prev[...])
    folded = folded + tdot(spread(t3, 8, t3_end, 8), a_next[256:512, :])
    for v in range(4):
        score = score + folded[32 * v:32 * v + 32, :]
    out[...] = score


def per_device(count_all, snps, genotypes, annotations, window_start, window_end):
    dma = pltpu.SemaphoreType.DMA
    vm = pltpu.VMEM
    any_spec = pl.BlockSpec(memory_space=pltpu.HBM)
    vmem_spec = pl.BlockSpec(memory_space=pltpu.VMEM)
    return pl.pallas_call(
        functools.partial(kernel, count_all, snps),
        out_shape=jax.ShapeDtypeStruct((32, 512), F32),
        in_specs=[any_spec, any_spec, any_spec, any_spec],
        out_specs=vmem_spec,
        scratch_shapes=[
            vm((2048, 512), BF16), vm((2048, 256), BF16), vm((2048, 256), BF16),
            vm((512, 512), BF16), vm((512, 512), BF16), vm((512, 512), BF16),
            *[vm((n, b, 32, 128), kind) for kind in (BF16, F32, BF16, BF16) for n, b in ((16, 4), (16, 2), (8, 2))],
            *[vm((8, b, 32, 128), BF16) for b in (4, 2, 2)],
            *[vm((b, 32, 128), F32) for b in (4, 2, 2)], vm((32, 512), F32), vm((128, 512), F32),
            vm((1, 512), F32), vm((16, 1, 512), F32), vm((1, 512), F32), vm((2, 1, 512), F32),
            vm((16, 8, 128), BF16), vm((8, 8, 128), BF16), vm((8, 8, 128), BF16),
            vm((16, 8, 128), BF16), vm((16, 8, 128), BF16), vm((8, 8, 128), BF16),
            vm((1, 32), jnp.int32), vm((1, 32), jnp.int32), dma((2,)),
            dma, dma, dma((4,)), dma((4,)), pltpu.SemaphoreType.REGULAR((3,)),
            dma((16,)), dma((16,)), dma((2,)), dma((2,)),
            dma((3, 16)), dma((3, 16)), dma((3, 8)), dma((3, 8)),
            dma((3, 16)), dma((16,)), dma((16,)), dma((8,)),
        ],
        compiler_params=pltpu.CompilerParams(
            collective_id=0, has_side_effects=True, vmem_limit_bytes=67043328),
        name="ld_scores",
    )(genotypes, annotations, window_start.reshape(1, 32), window_end.reshape(1, 32))


def solution(mesh):
    snps, groups = mesh.shape["snp"], mesh.shape["ind"]
    body = functools.partial(per_device, float(2048 * groups), snps)
    in_specs = (P("ind", "snp"), P("snp", None), P(("snp", "ind")), P(("snp", "ind")))
    return jax.shard_map(
        body, mesh=mesh, in_specs=in_specs, out_specs=P(("snp", "ind"), None), check_vma=False)
```
